32 devices in a mesh: lat: 8 (over y, x, core), chan: 4 (over z).
Axes of the slice: x: 2, y: 2, z: 4, core: 2. Of those that a mesh axis runs over, the one named last changes fastest.
Arguments:
- state: bfloat16 [256, 64, 1440], P('chan', 'lat'), may hold values from -6 to 6
- kernel: bfloat16 [3, 3, 256, 256], replicated, may hold values from -0.125 to 0.125
- bias: float32 [256], P('chan'), may hold values from -3 to 3
- innovations: float32 [256, 8, 8, 1024], P('chan', 'lat'), may hold values from -6 to 6
- interp: bfloat16 [4, 8, 8, 1024], P(None, 'lat'), may hold values from 0 to 1
- cells: int32 [8, 8, 1024], P('lat'), may hold values from 0 to 90719, as said below
- counts: int32 [8, 8], P('lat'), may hold values from 1 to 1024, as said below
Outputs:
- grad_state: bfloat16 [256, 64, 1440], P('chan', 'lat')
- departures: float32 [256, 8, 8, 1024], P('chan', 'lat')
The draws below stay inside these ranges and needn't reach their ends.
Inputs may be any that keep to these rules, and one draw needn't show every extreme that they name: `cells`: every observation of slab d has its first corner in rows 8 d to 8 d + 6. `counts`: in every draw some slab receives 1024 used slots from every instrument shard.
All inputs are finite; a program needn't handle non-finite values.
Results may differ from the reference program's by a relative error of at most 0.023.
Values may be sent and summed in bfloat16 or wider, within the bound.
No kernel may reach another device: no remote copies, remote signals or barrier semaphores. Data moves between devices by JAX's collectives and lax.ppermute only.
A program may use at most 256 MiB of HBM per device.

```python
import jax
import jax.numpy as jnp
from jax import lax

C = 256
LON = 1440
KERNEL_SPACING = 8
ROWS = 8
CAP = 1024
HEIGHT = 64
N_LAT = 8
N_CHAN = 4


def draw_cells(key, part):
    key_row = jax.random.fold_in(key, 11)
    key_col = jax.random.fold_in(key, 12)
    shape = (N_LAT, N_LAT, CAP)
    local_row = jax.random.randint(key_row, shape, 0, ROWS - 1, dtype=jnp.int32)
    column = jax.random.randint(key_col, shape, 0, LON, dtype=jnp.int32)
    slab = jnp.arange(N_LAT, dtype=jnp.int32)[None, :, None]
    return (slab * ROWS + local_row) * LON + column


def draw_counts(key, part):
    key_level = jax.random.fold_in(key, 21)
    key_peak = jax.random.fold_in(key, 22)
    key_jitter = jax.random.fold_in(key, 23)
    table = jnp.array([1, 2, 5, 10], dtype=jnp.int32)
    choose = jax.random.randint(key_level, (N_LAT,), 0, 4, dtype=jnp.int32)
    level = jnp.take(table, choose)
    peak = jax.random.randint(key_peak, (), 0, N_LAT, dtype=jnp.int32)
    slabs = jnp.arange(N_LAT, dtype=jnp.int32)
    level = jnp.where(slabs == peak, 10, level)
    jitter = jax.random.randint(key_jitter, (N_LAT, N_LAT), 0, max(CAP // 16, 1), dtype=jnp.int32)
    jitter = jnp.where(slabs[None, :] == peak, 0, jitter)
    return jnp.maximum(1, CAP * level[None, :] // 10 - jitter)


def levels(stream_key, dims, cuts, least, high):
    gain, own = 1.0, jax.random.fold_in(stream_key, 6)
    for dim, parts in cuts:
        draws = jnp.exp(jax.random.uniform(jax.random.fold_in(own, dim), (parts,), jnp.float32, least / len(cuts), high / len(cuts)))
        gain = gain * jnp.repeat(draws, dims[dim] // parts).reshape([-1 if axis == dim else 1 for axis in range(len(dims))])
    return gain


def centred(key, extent, scale, most, shards=(), kind=jnp.bfloat16):
    loudness = levels(key, extent, shards, -0.22, 0.18) if shards else 1.0
    entries = jax.random.normal(key, extent, jnp.float32) * scale * loudness
    return jnp.minimum(jnp.maximum(entries, -most), most).astype(kind)


def setup_inputs(seed: int = 0) -> dict:
    key_of = jax.random.split(jax.random.key(seed), 8)
    return {
        "state": centred(key_of[0], (C, HEIGHT, LON), 1.0, 6.0, ((0, 4), (1, 8))),
        "kernel": centred(key_of[1], (3, 3, C, C), (9 * C) ** -0.5, 0.125),
        "bias": centred(key_of[2], (C,), 0.5, 3.0, ((0, 4),), jnp.float32),
        "innovations": centred(key_of[3], (C, N_LAT, N_LAT, CAP), 1.0, 6.0, ((0, 4), (1, 8)), jnp.float32),
        "interp": jnp.clip(1.0 * jax.random.uniform(key_of[4], (4, N_LAT, N_LAT, CAP), jnp.float32) ** levels(key_of[4], (4, N_LAT, N_LAT, CAP), ((1, 8),), -0.2, 0.2), 0.0, 1.0).astype(jnp.bfloat16),
        "cells": draw_cells(jax.random.fold_in(key_of[7], 71), 0),
        "counts": draw_counts(jax.random.fold_in(key_of[7], 71), 0),
    }


def gelu_value(value):
    return 0.5 * value * (1.0 + jax.scipy.special.erf(value * 0.7071067811865476))


def gelu_slope(value):
    return 0.5 * (1.0 + jax.scipy.special.erf(value * 0.7071067811865476)) + value * jnp.exp(-0.5 * value * value) * 0.3989422804014327


def shifted_grid(grid_field, row_count, cols):
    field_height = grid_field.shape[1]
    padded_field = jnp.pad(grid_field, ((0, 0), (KERNEL_SPACING, KERNEL_SPACING), (0, 0)))
    part = lax.slice_in_dim(padded_field, KERNEL_SPACING + row_count, KERNEL_SPACING + row_count + field_height, axis=1)
    return jnp.roll(part, -cols, axis=2)


def channel_mix(grid_field, kernel_t, direction_sign):
    group = C // N_CHAN
    field_height = grid_field.shape[1]
    total = jnp.zeros((C, field_height * LON), jnp.float32)
    for index in range(N_CHAN):
        source_field = grid_field[index * group:(index + 1) * group].astype(jnp.float32)
        field_pieces = []
        for row_offset in range(3):
            for column_offset in range(3):
                field_pieces.append(shifted_grid(source_field, direction_sign * (row_offset - 1) * KERNEL_SPACING, direction_sign * (column_offset - 1) * KERNEL_SPACING))
        stacked = jnp.stack(field_pieces).reshape(9 * group, field_height * LON)
        weights = kernel_t[:, :, :, index * group:(index + 1) * group].astype(jnp.float32).reshape(C, 9 * group)
        part = jnp.dot(weights, stacked, preferred_element_type=jnp.float32)
        rounded = lax.optimization_barrier(part.astype(jnp.bfloat16))
        total = total + rounded.astype(jnp.float32)
    return total.reshape(C, field_height, LON)


def reference(state, kernel, bias, innovations, interp, cells, counts):
    forward_kernel = jnp.transpose(kernel, (2, 0, 1, 3))
    backward_kernel = jnp.transpose(kernel, (3, 0, 1, 2))
    pre = channel_mix(state, forward_kernel, 1) + bias[:, None, None]
    hidden = gelu_value(pre)
    flat_hidden = hidden.reshape(C, -1)
    slots = jnp.arange(innovations.shape[3], dtype=jnp.int32)
    mask = (slots[None, None, :] < counts[:, :, None]).astype(jnp.float32)
    weights = interp.astype(jnp.float32) * mask[None]
    row_index = cells // LON
    col_index = cells % LON
    corner_one = row_index * LON + (col_index + 1) % LON
    corners = [cells, corner_one, cells + LON, corner_one + LON]
    model = jnp.zeros(innovations.shape, jnp.float32)
    for which in range(4):
        model = model + weights[which][None] * jnp.take(flat_hidden, corners[which], axis=1)
    departures = model - innovations * mask[None]
    grad_hidden = jnp.zeros((C, flat_hidden.shape[1]), jnp.float32)
    for which in range(4):
        grad_hidden = grad_hidden.at[:, corners[which].reshape(-1)].add((weights[which][None] * departures).reshape(C, -1))
    grad_pre = (grad_hidden.reshape(pre.shape) * gelu_slope(pre)).astype(jnp.bfloat16)
    grad_state = channel_mix(grad_pre, backward_kernel, -1).astype(jnp.bfloat16)
    return grad_state, departures
```

```python
import functools

import jax
import jax.numpy as jnp
from jax import lax
from jax.experimental import pallas as pl
from jax.experimental.pallas import tpu as pltpu
from jax.sharding import PartitionSpec as P

SPACING = 8
LANES = 128
STEP = 120
TOGETHER = 4
OBS = 256

VMEM = pl.BlockSpec(memory_space=pltpu.VMEM)
SMEM = pl.BlockSpec(memory_space=pltpu.SMEM)
PARAMS = pltpu.CompilerParams(vmem_limit_bytes=56 * 1024 * 1024)


def padded_width(width):
    return -(-(width + 3 * SPACING) // LANES) * LANES


def lane_iota(shape):
    return lax.broadcasted_iota(jnp.int32, shape, len(shape) - 1)


def wrapped_tail(first, tail, rem):
    lane = lane_iota(tail.shape)
    head = pltpu.roll(first, rem, 1)
    end = pltpu.roll(tail, LANES - rem, 1)
    out = jnp.where(lane < rem, tail, jnp.where(lane < rem + 2 * SPACING, head, 0.0))
    return jnp.where(lane >= LANES - SPACING, end, out)


def split_rows_kernel(parts, rounds, place_ref, state_ref, *refs):
    outs, rows_ref = refs[:-1], refs[-1]
    group, rows, width = state_ref.shape
    wide = outs[0].shape[1]
    main = width // LANES * LANES
    rem = width - main
    place = place_ref[0]
    tiles = wide // LANES
    for tile in range(tiles):
        size = min(LANES, width - tile * LANES)
        part = state_ref[:, :, tile * LANES:tile * LANES + size].astype(jnp.float32)
        rows_ref[tile, :, :size] = part.reshape(group * rows, size)
    for turn in range(rounds):
        for k in range(parts):
            row = turn * parts + (place ^ k)
            out = outs[turn * parts + k]
            strips = [rows_ref[tile, pl.ds(row, group, stride=rows), :] for tile in range(tiles)]
            for tile in range(tiles - 1):
                out[:, tile * LANES:(tile + 1) * LANES] = strips[tile].astype(jnp.bfloat16)
            out[:, main:] = wrapped_tail(strips[0], strips[-1], rem).astype(jnp.bfloat16)


def split_rows(place, state, parts, wide):
    group, rows, width = state.shape
    rounds = rows // parts
    return pl.pallas_call(
        functools.partial(split_rows_kernel, parts, rounds),
        out_shape=[jax.ShapeDtypeStruct((group, wide), jnp.bfloat16)] * rows,
        in_specs=[SMEM, VMEM],
        out_specs=[VMEM] * rows,
        scratch_shapes=[pltpu.VMEM((wide // LANES, group * rows, LANES), jnp.float32)],
        compiler_params=PARAMS,
        name="split_rows",
    )(place, state)


def join_rows_kernel(parts, rounds, place_ref, *refs):
    pieces, out_ref, rows_ref = refs[:-2], refs[-2], refs[-1]
    group, rows, width = out_ref.shape
    place = place_ref[0]
    for turn in range(rounds):
        for k in range(parts):
            row = turn * parts + (place ^ k)
            piece = pieces[turn * parts + k]
            for tile in range(rows_ref.shape[0]):
                part = piece[:, tile * LANES:(tile + 1) * LANES].astype(jnp.float32)
                rows_ref[tile, pl.ds(row, group, stride=rows), :] = part
    for tile in range(rows_ref.shape[0]):
        size = min(LANES, width - tile * LANES)
        part = rows_ref[tile, :, :size].reshape(group, rows, size)
        out_ref[:, :, tile * LANES:tile * LANES + size] = part.astype(jnp.bfloat16)


def join_rows(place, pieces, parts, width):
    group, wide = pieces[0].shape
    rows = len(pieces)
    return pl.pallas_call(
        functools.partial(join_rows_kernel, parts, rows // parts),
        out_shape=jax.ShapeDtypeStruct((group, rows, width), jnp.bfloat16),
        in_specs=[SMEM] + [VMEM] * rows,
        out_specs=VMEM,
        scratch_shapes=[pltpu.VMEM((wide // LANES, group * rows, LANES), jnp.float32)],
        compiler_params=PARAMS,
        name="join_rows",
    )(place, *pieces)


def assemble_kernel(place_ref, *refs):
    pieces, out_ref = refs[:-1], refs[-1]
    group = pieces[0].shape[0]
    for k, piece in enumerate(pieces):
        start = pl.multiple_of((place_ref[0] ^ k) * group, group)
        out_ref[pl.ds(start, group), :] = piece[...]


def assemble(place, pieces):
    group, wide = pieces[0].shape
    return pl.pallas_call(
        assemble_kernel,
        out_shape=jax.ShapeDtypeStruct((group * len(pieces), wide), jnp.bfloat16),
        in_specs=[SMEM] + [VMEM] * len(pieces),
        out_specs=VMEM,
        compiler_params=PARAMS,
        name="assemble",
    )(place, *pieces)


def conv_kernel(place_ref, weights_ref, below_ref, here_ref, above_ref, *refs):
    outs, sums_ref = refs[:-1], refs[-1]
    group, wide = outs[0].shape
    total = here_ref.shape[0]
    columns = 2 * LANES

    @pl.loop(0, wide // columns)
    def _(tile):
        at = pl.ds(pl.multiple_of(tile * columns, columns), columns)
        part = jnp.dot(weights_ref[1], here_ref[:, at], preferred_element_type=jnp.float32)
        part += jnp.dot(weights_ref[0], below_ref[:, at], preferred_element_type=jnp.float32)
        part += jnp.dot(weights_ref[2], above_ref[:, at], preferred_element_type=jnp.float32)
        sums_ref[:, at] = part

    for k, out in enumerate(outs):
        start = (place_ref[0] ^ k) * group
        left = sums_ref[pl.ds(pl.multiple_of(start, group), group), :]
        middle = sums_ref[pl.ds(pl.multiple_of(start + total, group), group), :]
        right = sums_ref[pl.ds(pl.multiple_of(start + 2 * total, group), group), :]
        mixed = middle + pltpu.roll(left, SPACING, 1) + pltpu.roll(right, wide - SPACING, 1)
        out[...] = mixed.astype(jnp.bfloat16)


def conv(place, weights, below, here, above, parts):
    total, wide = here.shape
    group = total // parts
    return pl.pallas_call(
        conv_kernel,
        out_shape=[jax.ShapeDtypeStruct((group, wide), jnp.bfloat16)] * parts,
        in_specs=[SMEM] + [VMEM] * 4,
        out_specs=[VMEM] * parts,
        scratch_shapes=[pltpu.VMEM((3 * total, wide), jnp.float32)],
        compiler_params=PARAMS,
        cost_estimate=pl.CostEstimate(
            flops=18 * total * total * wide, bytes_accessed=8 * total * wide + 18 * total * total, transcendentals=0
        ),
        name="conv",
    )(place, weights, below, here, above)


def pack_obs_kernel(width, place_ref, counts_ref, values_ref, weights_ref, cells_ref, *refs):
    outs, tiles_ref = refs[:-1], refs[-1]
    slabs = len(outs)
    group = values_ref.shape[0] // slabs
    slots = values_ref.shape[1]
    blocks = -(-width // STEP)
    for tile in range(slots // LANES):
        tiles_ref[tile] = values_ref[:, tile * LANES:(tile + 1) * LANES]
    for k, out in enumerate(outs):
        slab = place_ref[0] ^ k
        used = lane_iota((1, slots)) < counts_ref[0, slab]
        values = jnp.concatenate(
            [tiles_ref[tile, pl.ds(slab, group, stride=slabs), :] for tile in range(slots // LANES)], axis=1
        )
        out[:group, :] = jnp.where(used, values, 0.0).astype(jnp.bfloat16)
        weights = jnp.where(used, weights_ref[slab], 0.0)
        local = (cells_ref[slab] - slab * (SPACING * width)).astype(jnp.float32)
        row = jnp.clip(jnp.floor((local + 0.5) * (1.0 / width)), 0.0, SPACING - 2.0)
        column = local - row * width
        block = jnp.clip(jnp.floor((column + 0.5) * (1.0 / STEP)), 0.0, blocks - 1.0)
        tail = jnp.concatenate(
            [weights, row * blocks + block, column - block * STEP, jnp.zeros((10, slots), jnp.float32)], axis=0
        )
        out[group:, :] = tail.astype(jnp.bfloat16)


def pack_obs(place, counts, values, weights, cells, width):
    group, slabs, slots = values.shape
    return pl.pallas_call(
        functools.partial(pack_obs_kernel, width),
        out_shape=[jax.ShapeDtypeStruct((group + 16, slots), jnp.bfloat16)] * slabs,
        in_specs=[SMEM, SMEM, VMEM, VMEM, VMEM],
        out_specs=[VMEM] * slabs,
        scratch_shapes=[pltpu.VMEM((slots // LANES, group * slabs, LANES), jnp.float32)],
        compiler_params=PARAMS,
        name="pack_obs",
    )(place, counts, values.reshape(group * slabs, slots), weights, cells)


def unpack_obs_kernel(place_ref, *refs):
    pieces, out_ref, tiles_ref = refs[:-2], refs[-2], refs[-1]
    slabs = len(pieces)
    group = out_ref.shape[0] // slabs
    for k, piece in enumerate(pieces):
        slab = place_ref[0] ^ k
        for tile in range(tiles_ref.shape[0]):
            part = piece[:, tile * LANES:(tile + 1) * LANES].astype(jnp.float32)
            tiles_ref[tile, pl.ds(slab, group, stride=slabs), :] = part
    for tile in range(tiles_ref.shape[0]):
        out_ref[:, tile * LANES:(tile + 1) * LANES] = tiles_ref[tile]


def unpack_obs(place, pieces):
    group, slots = pieces[0].shape
    slabs = len(pieces)
    return pl.pallas_call(
        unpack_obs_kernel,
        out_shape=jax.ShapeDtypeStruct((group * slabs, slots), jnp.float32),
        in_specs=[SMEM] + [VMEM] * slabs,
        out_specs=VMEM,
        scratch_shapes=[pltpu.VMEM((slots // LANES, group * slabs, LANES), jnp.float32)],
        compiler_params=PARAMS,
        name="unpack_obs",
    )(place, *pieces)


def gelu_value(value):
    return 0.5 * value * (1.0 + lax.erf(value * 0.7071067811865476))


def gelu_slope(value):
    return (
        0.5 * (1.0 + lax.erf(value * 0.7071067811865476))
        + value * jnp.exp(-0.5 * value * value) * 0.3989422804014327
    )


def observe_kernel(parts, rounds, slabs, width, place_ref, bias_ref, *refs):
    rows = parts * rounds
    mixed, obs = refs[:rows], refs[rows:rows + slabs]
    grads = refs[rows + slabs:2 * rows + slabs]
    departures = refs[2 * rows + slabs:2 * rows + 2 * slabs]
    pre_ref, table_ref, found_ref, row_ref = refs[2 * rows + 2 * slabs:]
    group, wide = mixed[0].shape
    slots = obs[0].shape[1]
    blocks = -(-width // STEP)
    tiles = wide // LANES
    place = place_ref[0]
    rem = width % LANES
    last = width // LANES
    lane = lane_iota((group, LANES))
    bias = bias_ref[...]

    for turn in range(rounds):
        for k in range(parts):
            row = turn * parts + (place ^ k)
            pre_ref[row] = mixed[turn * parts + k][...].astype(jnp.float32) + bias

    @pl.loop(0, rows)
    def _(row):
        row_ref[...] = gelu_value(pre_ref[row])
        for j in range(blocks):
            tile, shift = divmod(j * STEP, LANES)
            block = row_ref[:, tile * LANES:(tile + 1) * LANES]
            if shift:
                after = row_ref[:, (tile + 1) * LANES:(tile + 2) * LANES]
                block = jnp.where(
                    lane < LANES - shift,
                    pltpu.roll(block, LANES - shift, 1),
                    pltpu.roll(after, LANES - shift, 1),
                )
            block = block.astype(jnp.bfloat16)

            @pl.when(row < rows - 1)
            def _():
                at = pl.multiple_of((row * blocks + j) * group, group)
                table_ref[pl.ds(at, group), :LANES] = block

            @pl.when(row > 0)
            def _():
                at = pl.multiple_of(((row - 1) * blocks + j) * group, group)
                table_ref[pl.ds(at, group), LANES:] = block

    found_ref[...] = jnp.zeros_like(found_ref)
    steps = (rows - 1) * blocks // TOGETHER
    high = TOGETHER * group
    lo_iota = lax.broadcasted_iota(jnp.int32, (LANES, OBS), 0)
    for s in range(slabs):
        @pl.loop(0, slots // OBS)
        def _(sub):
            at = pl.ds(pl.multiple_of(sub * OBS, OBS), OBS)
            side = obs[s][group:, at].astype(jnp.float32)
            which = side[4:5].astype(jnp.int32)
            low = side[5:6].astype(jnp.int32)
            first, second = lo_iota == low, lo_iota == low + 1
            spread = jnp.concatenate(
                [
                    jnp.where(first, side[0:1], jnp.where(second, side[1:2], 0.0)),
                    jnp.where(first, side[2:3], jnp.where(second, side[3:4], 0.0)),
                ],
                axis=0,
            ).astype(jnp.bfloat16)
            whole = jnp.broadcast_to(which, (group, OBS))

            def gather(step, model):
                start = pl.multiple_of(step * high, high)
                part = jnp.dot(table_ref[pl.ds(start, high), :], spread, preferred_element_type=jnp.float32)
                for i in range(TOGETHER):
                    model = jnp.where(whole == step * TOGETHER + i, part[i * group:(i + 1) * group], model)
                return model

            model = lax.fori_loop(0, steps, gather, jnp.zeros((group, OBS), jnp.float32))
            departure = model - obs[s][:group, at].astype(jnp.float32)
            departures[s][:, at] = departure.astype(jnp.bfloat16)

            @pl.loop(0, steps)
            def _(step):
                start = pl.multiple_of(step * high, high)
                chosen = jnp.concatenate(
                    [jnp.where(whole == step * TOGETHER + i, departure, 0.0) for i in range(TOGETHER)], axis=0
                ).astype(jnp.bfloat16)
                found_ref[pl.ds(start, high), :] += lax.dot_general(
                    chosen, spread, (((1,), (1,)), ((), ())), preferred_element_type=jnp.float32
                )

    for turn in range(rounds):
        for k in range(parts):
            row = turn * parts + (place ^ k)
            out = grads[turn * parts + k]
            sums = [jnp.zeros((group, LANES), jnp.float32) for _ in range(tiles)]
            upper = pl.multiple_of(jnp.minimum(row, rows - 2) * (blocks * group), group)
            lower = pl.multiple_of(jnp.maximum(row - 1, 0) * (blocks * group), group)
            has_upper = row < rows - 1
            has_lower = row > 0
            for j in range(blocks):
                tile, shift = divmod(j * STEP, LANES)
                top = found_ref[pl.ds(upper + j * group, group), :LANES]
                low = found_ref[pl.ds(lower + j * group, group), LANES:]
                block = jnp.where(has_upper, top, 0.0) + jnp.where(has_lower, low, 0.0)
                if shift:
                    block = pltpu.roll(block, shift, 1)
                    sums[tile] += jnp.where(lane >= shift, block, 0.0)
                    sums[tile + 1] += jnp.where(lane < shift, block, 0.0)
                else:
                    sums[tile] += block
            sums[0] += jnp.where(lane == 0, pltpu.roll(sums[last], LANES - rem, 1), 0.0)
            for tile in range(tiles):
                at = slice(tile * LANES, (tile + 1) * LANES)
                sums[tile] *= gelu_slope(pre_ref[row, :, at])
                if tile < last:
                    out[:, at] = sums[tile].astype(jnp.bfloat16)
            out[:, last * LANES:] = wrapped_tail(sums[0], sums[last], rem).astype(jnp.bfloat16)


def observe(place, bias, mixed, obs, parts, width):
    group, wide = mixed[0].shape
    rows, slabs = len(mixed), len(obs)
    slots = obs[0].shape[1]
    blocks = -(-width // STEP)
    found = (rows - 1) * blocks * group
    results = pl.pallas_call(
        functools.partial(observe_kernel, parts, rows // parts, slabs, width),
        out_shape=[jax.ShapeDtypeStruct((group, wide), jnp.bfloat16)] * rows
        + [jax.ShapeDtypeStruct((group, slots), jnp.bfloat16)] * slabs,
        in_specs=[SMEM] + [VMEM] * (1 + rows + slabs),
        out_specs=[VMEM] * (rows + slabs),
        scratch_shapes=[
            pltpu.VMEM((rows, group, wide), jnp.float32),
            pltpu.VMEM((found, 2 * LANES), jnp.bfloat16),
            pltpu.VMEM((found, 2 * LANES), jnp.float32),
            pltpu.VMEM((group, wide), jnp.float32),
        ],
        compiler_params=PARAMS,
        name="observe",
    )(place, bias, *mixed, *obs)
    return results[:rows], results[rows:]


def swap(piece, axis, k):
    if k == 0:
        return piece
    return lax.ppermute(piece, axis, [(i, i ^ k) for i in range(lax.axis_size(axis))])


def mix(place, weights, pieces, parts):
    count = lax.axis_size("lat")
    forward = [(i, i + 1) for i in range(count - 1)]
    backward = [(i + 1, i) for i in range(count - 1)]
    results = []
    for turn in range(len(pieces) // parts):
        own = pieces[turn * parts:(turn + 1) * parts]
        here = assemble(place, [swap(own[k], "chan", k) for k in range(parts)])
        below = lax.ppermute(here, "lat", forward)
        above = lax.ppermute(here, "lat", backward)
        mixed = conv(place, weights, below, here, above, parts)
        results += [swap(mixed[k], "chan", k) for k in range(parts)]
    return results


def shards(state, kernel, bias, innovations, interp, cells, counts):
    group, rows, width = state.shape
    parts, slabs = lax.axis_size("chan"), lax.axis_size("lat")
    wide = padded_width(width)
    total = kernel.shape[2]
    chan_place = lax.axis_index("chan").reshape(1)
    lat_place = lax.axis_index("lat").reshape(1)
    forward_weights = kernel.reshape(3, 3 * total, total)
    backward_weights = jnp.transpose(kernel[::-1, ::-1], (0, 1, 3, 2)).reshape(3, 3 * total, total)

    mixed = mix(chan_place, forward_weights, split_rows(chan_place, state, parts, wide), parts)

    interp_rows = jnp.transpose(interp[:, 0], (1, 0, 2)).astype(jnp.float32)
    packed = pack_obs(
        lat_place, counts, innovations[:, 0], interp_rows, cells[0][:, None, :], width
    )
    obs = [swap(packed[k], "lat", k) for k in range(slabs)]

    grads, departures = observe(chan_place, bias[:, None], mixed, obs, parts, width)
    returned = [swap(departures[k], "lat", k) for k in range(slabs)]
    departures_out = unpack_obs(lat_place, returned).reshape(innovations.shape)
    grad_state = join_rows(chan_place, mix(chan_place, backward_weights, grads, parts), parts, width)
    return grad_state, departures_out


def solution(mesh):
    return jax.shard_map(
        shards,
        mesh=mesh,
        in_specs=(
            P("chan", "lat", None),
            P(),
            P("chan"),
            P("chan", "lat", None, None),
            P(None, "lat", None, None),
            P("lat", None, None),
            P("lat", None),
        ),
        out_specs=(P("chan", "lat", None), P("chan", "lat", None, None)),
        check_vma=False,
    )
```

```python
import functools

import jax
import jax.numpy as jnp
from jax import lax
from jax.experimental import pallas as pl
from jax.experimental.pallas import tpu as pltpu
from jax.sharding import PartitionSpec as P

SPACING = 8
LANES = 128
STEP = 120
WINDOW = 12
OBS = 256
SIDE = 16
JOIN = 2

VMEM = pl.BlockSpec(memory_space=pltpu.VMEM)
SMEM = pl.BlockSpec(memory_space=pltpu.SMEM)
SMALL = pl.CostEstimate(flops=1000, bytes_accessed=1000, transcendentals=0)
PARAMS = pltpu.CompilerParams(vmem_limit_bytes=56 * 1024 * 1024)


def padded_width(width):
    return -(-(width + 3 * SPACING) // LANES) * LANES


def lane_iota(shape):
    return lax.broadcasted_iota(jnp.int32, shape, len(shape) - 1)


def wrapped_tail(first, tail, rem):
    lane = lane_iota(tail.shape)
    head = pltpu.roll(first, rem, 1)
    end = pltpu.roll(tail, LANES - rem, 1)
    out = jnp.where(lane < rem, tail, jnp.where(lane < rem + 2 * SPACING, head, 0.0))
    return jnp.where(lane >= LANES - SPACING, end, out)


def split_rows_kernel(parts, rounds, place_ref, state_ref, *refs):
    outs, rows_ref = refs[:-1], refs[-1]
    group, rows, width = state_ref.shape
    wide = outs[0].shape[1]
    main = width // LANES * LANES
    rem = width - main
    place = place_ref[0]
    tiles = wide // LANES
    for tile in range(tiles):
        size = min(LANES, width - tile * LANES)
        part = state_ref[:, :, tile * LANES:tile * LANES + size].astype(jnp.float32)
        rows_ref[tile, :, :size] = part.reshape(group * rows, size)
    for turn in range(rounds):
        for k in range(parts):
            row = turn * parts + (place ^ k)
            out = outs[turn * parts + k]
            strips = [rows_ref[tile, pl.ds(row, group, stride=rows), :] for tile in range(tiles)]
            for tile in range(tiles - 1):
                out[:, tile * LANES:(tile + 1) * LANES] = strips[tile].astype(jnp.bfloat16)
            out[:, main:] = wrapped_tail(strips[0], strips[-1], rem).astype(jnp.bfloat16)


def split_rows(place, state, parts, wide):
    group, rows, width = state.shape
    rounds = rows // parts
    return pl.pallas_call(
        functools.partial(split_rows_kernel, parts, rounds),
        out_shape=[jax.ShapeDtypeStruct((group, wide), jnp.bfloat16)] * rows,
        in_specs=[SMEM, VMEM],
        out_specs=[VMEM] * rows,
        scratch_shapes=[pltpu.VMEM((wide // LANES, group * rows, LANES), jnp.float32)],
        compiler_params=PARAMS,
        cost_estimate=SMALL,
        name="split_rows",
    )(place, state)


def join_rows_kernel(parts, rounds, place_ref, *refs):
    pieces, out_ref, rows_ref = refs[:-2], refs[-2], refs[-1]
    group, rows, width = out_ref.shape
    place = place_ref[0]
    for turn in range(rounds):
        for k in range(parts):
            row = turn * parts + (place ^ k)
            piece = pieces[turn * parts + k]
            for tile in range(rows_ref.shape[0]):
                part = piece[:, tile * LANES:(tile + 1) * LANES].astype(jnp.float32)
                rows_ref[tile, pl.ds(row, group, stride=rows), :] = part
    for tile in range(rows_ref.shape[0]):
        size = min(LANES, width - tile * LANES)
        part = rows_ref[tile, :, :size].reshape(group, rows, size)
        out_ref[:, :, tile * LANES:tile * LANES + size] = part.astype(jnp.bfloat16)


def join_rows(place, pieces, parts, width):
    group, wide = pieces[0].shape
    rows = len(pieces)
    return pl.pallas_call(
        functools.partial(join_rows_kernel, parts, rows // parts),
        out_shape=jax.ShapeDtypeStruct((group, rows, width), jnp.bfloat16),
        in_specs=[SMEM] + [VMEM] * rows,
        out_specs=VMEM,
        scratch_shapes=[pltpu.VMEM((wide // LANES, group * rows, LANES), jnp.float32)],
        compiler_params=PARAMS,
        cost_estimate=SMALL,
        name="join_rows",
    )(place, *pieces)


def assemble_kernel(place_ref, *refs):
    pieces, out_ref = refs[:-1], refs[-1]
    group = pieces[0].shape[0]
    for k, piece in enumerate(pieces):
        start = pl.multiple_of((place_ref[0] ^ k) * group, group)
        out_ref[pl.ds(start, group), :] = piece[...]


def assemble(place, pieces):
    group, wide = pieces[0].shape
    return pl.pallas_call(
        assemble_kernel,
        out_shape=jax.ShapeDtypeStruct((group * len(pieces), wide), jnp.bfloat16),
        in_specs=[SMEM] + [VMEM] * len(pieces),
        out_specs=VMEM,
        compiler_params=PARAMS,
        cost_estimate=SMALL,
        name="assemble",
    )(place, *pieces)


def conv_kernel(place_ref, weights_ref, below_ref, here_ref, above_ref, *refs):
    outs, sums_ref = refs[:-1], refs[-1]
    group, wide = outs[0].shape
    total = here_ref.shape[0]
    columns = 2 * LANES

    @pl.loop(0, wide // columns)
    def _(tile):
        at = pl.ds(pl.multiple_of(tile * columns, columns), columns)
        part = jnp.dot(weights_ref[1], here_ref[:, at], preferred_element_type=jnp.float32)
        part += jnp.dot(weights_ref[0], below_ref[:, at], preferred_element_type=jnp.float32)
        part += jnp.dot(weights_ref[2], above_ref[:, at], preferred_element_type=jnp.float32)
        sums_ref[:, at] = part

    for k, out in enumerate(outs):
        start = (place_ref[0] ^ k) * group
        left = sums_ref[pl.ds(pl.multiple_of(start, group), group), :]
        middle = sums_ref[pl.ds(pl.multiple_of(start + total, group), group), :]
        right = sums_ref[pl.ds(pl.multiple_of(start + 2 * total, group), group), :]
        mixed = middle + pltpu.roll(left, SPACING, 1) + pltpu.roll(right, wide - SPACING, 1)
        out[...] = mixed.astype(jnp.bfloat16)


def conv(place, weights, below, here, above, parts):
    total, wide = here.shape
    group = total // parts
    return pl.pallas_call(
        conv_kernel,
        out_shape=[jax.ShapeDtypeStruct((group, wide), jnp.bfloat16)] * parts,
        in_specs=[SMEM] + [VMEM] * 4,
        out_specs=[VMEM] * parts,
        scratch_shapes=[pltpu.VMEM((3 * total, wide), jnp.float32)],
        compiler_params=PARAMS,
        cost_estimate=SMALL,
        name="conv",
    )(place, weights, below, here, above)


def pack_obs_kernel(width, counts_ref, values_ref, weights_ref, cells_ref, out_ref, tiles_ref):
    slabs, depth, slots = out_ref.shape
    group = depth - SIDE
    blocks = -(-width // STEP)
    for tile in range(slots // LANES):
        tiles_ref[tile] = values_ref[:, tile * LANES:(tile + 1) * LANES]
    for slab in range(slabs):
        used = lane_iota((1, slots)) < counts_ref[0, slab]
        values = jnp.concatenate(
            [tiles_ref[tile, pl.ds(slab, group, stride=slabs), :] for tile in range(slots // LANES)], axis=1
        )
        out_ref[slab, :group, :] = jnp.where(used, values, 0.0).astype(jnp.bfloat16)
        weights = jnp.where(used, weights_ref[slab], 0.0)
        local = (cells_ref[slab] - slab * (SPACING * width)).astype(jnp.float32)
        row = jnp.clip(jnp.floor((local + 0.5) * (1.0 / width)), 0.0, SPACING - 2.0)
        column = local - row * width
        block = jnp.clip(jnp.floor((column + 0.5) * (1.0 / STEP)), 0.0, blocks - 1.0)
        side = jnp.concatenate(
            [weights, row * blocks + block, column - block * STEP, jnp.zeros((SIDE - 6, slots), jnp.float32)],
            axis=0,
        )
        out_ref[slab, group:, :] = side.astype(jnp.bfloat16)


def pack_obs(counts, values, weights, cells, width):
    group, slabs, slots = values.shape
    return pl.pallas_call(
        functools.partial(pack_obs_kernel, width),
        out_shape=jax.ShapeDtypeStruct((slabs, group + SIDE, slots), jnp.bfloat16),
        in_specs=[SMEM, VMEM, VMEM, VMEM],
        out_specs=VMEM,
        scratch_shapes=[pltpu.VMEM((slots // LANES, group * slabs, LANES), jnp.float32)],
        compiler_params=PARAMS,
        cost_estimate=SMALL,
        name="pack_obs",
    )(counts, values.reshape(group * slabs, slots), weights, cells)


def sort_obs_kernel(begin, obs_ref, sorted_ref, rank_ref, first_ref, last_ref, joined_ref, column_ref):
    sets, depth, size = sorted_ref.shape
    group = depth - SIDE
    each = obs_ref.shape[2]
    for s in range(sets):
        for i in range(size // each):
            joined_ref[:, i * each:(i + 1) * each] = obs_ref[begin + s * (size // each) + i]
        which = joined_ref[group:, :].astype(jnp.float32)[4:5]
        key = which * size + lane_iota((1, size)).astype(jnp.float32)
        column_ref[...] = jnp.transpose(jnp.broadcast_to(key, (LANES, size)))
        ranks = []
        for tile in range(size // LANES):
            below = jnp.where(column_ref[...] < key[:, tile * LANES:(tile + 1) * LANES], 1.0, 0.0)
            ranks.append(jnp.sum(below, axis=0, keepdims=True))
        rank = jnp.concatenate(ranks, axis=1)
        rank_ref[s] = rank.astype(jnp.int32)
        column_ref[...] = jnp.transpose(jnp.broadcast_to(rank, (LANES, size)))

        @pl.loop(0, size // OBS)
        def _(tile):
            start = pl.multiple_of(tile * OBS, OBS)
            chosen = []
            for i in range(OBS // LANES):
                order = (lane_iota((1, LANES)) + (start + i * LANES)).astype(jnp.float32)
                chosen.append(jnp.where(column_ref[...] == order, 1.0, 0.0).astype(jnp.bfloat16))
            taken = jnp.dot(
                joined_ref[...], jnp.concatenate(chosen, axis=1), preferred_element_type=jnp.float32
            )
            sorted_ref[s, :, pl.ds(start, OBS)] = taken.astype(jnp.bfloat16)
            which = taken[group + 4:group + 5]
            first_ref[s * (size // OBS) + tile] = jnp.min(which).astype(jnp.int32)
            last_ref[s * (size // OBS) + tile] = jnp.max(which).astype(jnp.int32)


def sort_obs(obs, begin, slabs):
    depth, slots = obs.shape[1:]
    size = slots * JOIN
    sets = slabs // JOIN
    return pl.pallas_call(
        functools.partial(sort_obs_kernel, begin),
        out_shape=[
            jax.ShapeDtypeStruct((sets, depth, size), jnp.bfloat16),
            jax.ShapeDtypeStruct((sets, 1, size), jnp.int32),
            jax.ShapeDtypeStruct((sets * size // OBS,), jnp.int32),
            jax.ShapeDtypeStruct((sets * size // OBS,), jnp.int32),
        ],
        in_specs=[VMEM],
        out_specs=[VMEM, VMEM, SMEM, SMEM],
        scratch_shapes=[pltpu.VMEM((depth, size), jnp.bfloat16), pltpu.VMEM((size, LANES), jnp.float32)],
        compiler_params=PARAMS,
        cost_estimate=SMALL,
        name="sort_obs",
    )(obs)


def unsort_obs_kernel(sorted_ref, one_ref, two_ref, out_ref):
    sets, group, size = sorted_ref.shape
    each = out_ref.shape[2]
    for s in range(sets):
        @pl.loop(0, size // OBS)
        def _(tile):
            start = pl.multiple_of(tile * OBS, OBS)
            rank = (one_ref if s < sets // 2 else two_ref)[s % (sets // 2), :, pl.ds(start, OBS)]
            chosen = jnp.where(lax.broadcasted_iota(jnp.int32, (size, OBS), 0) == rank, 1.0, 0.0)
            taken = jnp.dot(sorted_ref[s], chosen.astype(jnp.bfloat16), preferred_element_type=jnp.float32)
            slab = s * (size // each) + tile // (each // OBS)
            at = pl.ds(pl.multiple_of(tile % (each // OBS) * OBS, OBS), OBS)
            out_ref[slab, :, at] = taken.astype(jnp.bfloat16)


def unsort_obs(values, one, two, slabs):
    sets, group, size = values.shape
    return pl.pallas_call(
        unsort_obs_kernel,
        out_shape=jax.ShapeDtypeStruct((slabs, group, sets * size // slabs), jnp.bfloat16),
        in_specs=[VMEM] * 3,
        out_specs=VMEM,
        compiler_params=PARAMS,
        cost_estimate=SMALL,
        name="unsort_obs",
    )(values, one, two)


def unpack_obs_kernel(values_ref, out_ref, tiles_ref):
    slabs, group, slots = values_ref.shape
    for slab in range(slabs):
        for tile in range(slots // LANES):
            part = values_ref[slab, :, tile * LANES:(tile + 1) * LANES].astype(jnp.float32)
            tiles_ref[tile, pl.ds(slab, group, stride=slabs), :] = part
    for tile in range(slots // LANES):
        out_ref[:, tile * LANES:(tile + 1) * LANES] = tiles_ref[tile]


def unpack_obs(values):
    slabs, group, slots = values.shape
    return pl.pallas_call(
        unpack_obs_kernel,
        out_shape=jax.ShapeDtypeStruct((group * slabs, slots), jnp.float32),
        in_specs=[VMEM],
        out_specs=VMEM,
        scratch_shapes=[pltpu.VMEM((slots // LANES, group * slabs, LANES), jnp.float32)],
        compiler_params=PARAMS,
        cost_estimate=SMALL,
        name="unpack_obs",
    )(values)


def gelu_value(value):
    return 0.5 * value * (1.0 + lax.erf(value * 0.7071067811865476))


def gelu_slope(value):
    return (
        0.5 * (1.0 + lax.erf(value * 0.7071067811865476))
        + value * jnp.exp(-0.5 * value * value) * 0.3989422804014327
    )


def observe_kernel(parts, rounds, width, place_ref, *refs):
    rows = parts * rounds
    firsts, lasts, halves, bias_ref = refs[0:2], refs[2:4], refs[4:6], refs[6]
    mixed, grads, departure_ref = refs[7:7 + rows], refs[7 + rows:7 + 2 * rows], refs[7 + 2 * rows]
    pre_ref, table_ref, found_ref, row_ref, obs_ref, arrival = refs[8 + 2 * rows:]
    sets = obs_ref.shape[0] // 2
    copies = [
        pltpu.make_async_copy(half, obs_ref.at[pl.ds(i * sets, sets)], arrival.at[i])
        for i, half in enumerate(halves)
    ]
    for copy in copies:
        copy.start()
    group, wide = mixed[0].shape
    size = obs_ref.shape[2]
    blocks = -(-width // STEP)
    tiles = wide // LANES
    place = place_ref[0]
    rem = width % LANES
    last = width // LANES
    lane = lane_iota((group, LANES))
    bias = bias_ref[...]

    for turn in range(rounds):
        for k in range(parts):
            row = turn * parts + (place ^ k)
            pre_ref[row] = mixed[turn * parts + k][...].astype(jnp.float32) + bias

    @pl.loop(0, rows)
    def _(row):
        row_ref[...] = gelu_value(pre_ref[row])
        for j in range(blocks):
            tile, shift = divmod(j * STEP, LANES)
            block = row_ref[:, tile * LANES:(tile + 1) * LANES]
            if shift:
                after = row_ref[:, (tile + 1) * LANES:(tile + 2) * LANES]
                block = jnp.where(
                    lane < LANES - shift,
                    pltpu.roll(block, LANES - shift, 1),
                    pltpu.roll(after, LANES - shift, 1),
                )
            block = block.astype(jnp.bfloat16)

            @pl.when(row < rows - 1)
            def _():
                at = pl.multiple_of((row * blocks + j) * group, group)
                table_ref[pl.ds(at, group), :LANES] = block

            @pl.when(row > 0)
            def _():
                at = pl.multiple_of(((row - 1) * blocks + j) * group, group)
                table_ref[pl.ds(at, group), LANES:] = block

    found_ref[...] = jnp.zeros_like(found_ref)
    table_ref[(rows - 1) * blocks * group:, :] = jnp.zeros((WINDOW * group, 2 * LANES), jnp.bfloat16)
    high = WINDOW * group
    lo_iota = lax.broadcasted_iota(jnp.int32, (LANES, OBS), 0)

    for copy in copies:
        copy.wait()
    count = firsts[0].shape[0]

    @pl.loop(0, 2 * count)
    def _(number):
        s = number // (size // OBS)
        at = pl.ds(pl.multiple_of(number % (size // OBS) * OBS, OBS), OBS)
        side = obs_ref[s, group:, at].astype(jnp.float32)
        which = side[4:5].astype(jnp.int32)
        low = side[5:6].astype(jnp.int32)
        first, second = lo_iota == low, lo_iota == low + 1
        spread = jnp.concatenate(
            [
                jnp.where(first, side[0:1], jnp.where(second, side[1:2], 0.0)),
                jnp.where(first, side[2:3], jnp.where(second, side[3:4], 0.0)),
            ],
            axis=0,
        ).astype(jnp.bfloat16)
        whole = jnp.broadcast_to(which, (group, OBS))
        here, there = jnp.minimum(number, count - 1), jnp.maximum(number - count, 0)
        lowest = jnp.where(number < count, firsts[0][here], firsts[1][there])
        highest = jnp.where(number < count, lasts[0][here], lasts[1][there])
        lowest = jnp.clip(lowest, 0, (rows - 1) * blocks - 1)
        highest = jnp.clip(highest, 0, (rows - 1) * blocks - 1)
        windows = (highest - lowest) // WINDOW + 1

        def gather(window, model):
            base = lowest + window * WINDOW
            start = pl.multiple_of(base * group, group)
            part = jnp.dot(table_ref[pl.ds(start, high), :], spread, preferred_element_type=jnp.float32)
            for i in range(WINDOW):
                model = jnp.where(whole == base + i, part[i * group:(i + 1) * group], model)
            return model

        model = lax.fori_loop(0, windows, gather, jnp.zeros((group, OBS), jnp.float32))
        departure = model - obs_ref[s, :group, at].astype(jnp.float32)
        departure_ref[s, :, at] = departure.astype(jnp.bfloat16)

        @pl.loop(0, windows)
        def _(window):
            base = lowest + window * WINDOW
            start = pl.multiple_of(base * group, group)
            chosen = jnp.concatenate(
                [jnp.where(whole == base + i, departure, 0.0) for i in range(WINDOW)], axis=0
            ).astype(jnp.bfloat16)
            found_ref[pl.ds(start, high), :] += lax.dot_general(
                chosen, spread, (((1,), (1,)), ((), ())), preferred_element_type=jnp.float32
            )

    for turn in range(rounds):
        for k in range(parts):
            row = turn * parts + (place ^ k)
            out = grads[turn * parts + k]
            sums = [jnp.zeros((group, LANES), jnp.float32) for _ in range(tiles)]
            upper = pl.multiple_of(jnp.minimum(row, rows - 2) * (blocks * group), group)
            lower = pl.multiple_of(jnp.maximum(row - 1, 0) * (blocks * group), group)
            has_upper = row < rows - 1
            has_lower = row > 0
            for j in range(blocks):
                tile, shift = divmod(j * STEP, LANES)
                top = found_ref[pl.ds(upper + j * group, group), :LANES]
                low = found_ref[pl.ds(lower + j * group, group), LANES:]
                block = jnp.where(has_upper, top, 0.0) + jnp.where(has_lower, low, 0.0)
                if shift:
                    block = pltpu.roll(block, shift, 1)
                    sums[tile] += jnp.where(lane >= shift, block, 0.0)
                    sums[tile + 1] += jnp.where(lane < shift, block, 0.0)
                else:
                    sums[tile] += block
            sums[0] += jnp.where(lane == 0, pltpu.roll(sums[last], LANES - rem, 1), 0.0)
            for tile in range(tiles):
                at = slice(tile * LANES, (tile + 1) * LANES)
                sums[tile] *= gelu_slope(pre_ref[row, :, at])
                if tile < last:
                    out[:, at] = sums[tile].astype(jnp.bfloat16)
            out[:, last * LANES:] = wrapped_tail(sums[0], sums[last], rem).astype(jnp.bfloat16)


def observe(place, one, two, bias, mixed, parts, width):
    group, wide = mixed[0].shape
    rows = len(mixed)
    blocks = -(-width // STEP)
    found = ((rows - 1) * blocks + WINDOW) * group
    sets, depth, size = 2 * one[0].shape[0], one[0].shape[1], one[0].shape[2]
    results = pl.pallas_call(
        functools.partial(observe_kernel, parts, rows // parts, width),
        out_shape=[jax.ShapeDtypeStruct((group, wide), jnp.bfloat16)] * rows
        + [jax.ShapeDtypeStruct((sets, group, size), jnp.bfloat16)],
        in_specs=[SMEM] * 5 + [pl.BlockSpec(memory_space=pl.ANY)] * 2 + [VMEM] * (1 + rows),
        out_specs=[VMEM] * (rows + 1),
        scratch_shapes=[
            pltpu.VMEM((rows, group, wide), jnp.float32),
            pltpu.VMEM((found, 2 * LANES), jnp.bfloat16),
            pltpu.VMEM((found, 2 * LANES), jnp.float32),
            pltpu.VMEM((group, wide), jnp.float32),
            pltpu.VMEM((sets, depth, size), jnp.bfloat16),
            pltpu.SemaphoreType.DMA((2,)),
        ],
        compiler_params=PARAMS,
        cost_estimate=SMALL,
        name="observe",
    )(place, one[2], two[2], one[3], two[3], one[0], two[0], bias, *mixed)
    return results[:rows], results[rows]


def swap(piece, axis, k):
    if k == 0:
        return piece
    return lax.ppermute(piece, axis, [(i, i ^ k) for i in range(lax.axis_size(axis))])


def after(value, *others):
    return lax.optimization_barrier((value, *others))[0]


def mix(place, weights, pieces, parts, ahead=(), between=None):
    count = lax.axis_size("lat")
    forward = [(i, i + 1) for i in range(count - 1)]
    backward = [(i + 1, i) for i in range(count - 1)]
    results, done = [None] * len(pieces), ()
    turns = len(pieces) // parts
    here, arrived, halos, mixed = None, [None] * parts, ahead, None
    for turn in range(turns):
        own = list(pieces[turn * parts:(turn + 1) * parts])
        if turn:
            own[1:] = [after(own[k], arrived[k] if k > 1 else here) for k in range(1, parts)]
        arrived = [swap(own[k], "chan", k) for k in range(parts)]
        if between is not None and turn == min(1, turns - 1):
            done = between(here if turn else arrived[1])
            arrived[0] = after(arrived[0], *done)
        here = assemble(place, arrived)
        if halos:
            here = after(here, *halos)
        halos = [lax.ppermute(here, "lat", forward), lax.ppermute(here, "lat", backward)]
        ready = after(here, results[0]) if turn else here
        mixed = list(conv(place, weights, halos[0], ready, halos[1], parts))
        for k in range(parts):
            if turn and k:
                mixed[k] = after(mixed[k], results[(turn - 1) * parts + k])
            results[turn * parts + k] = swap(mixed[k], "chan", k)
    return results, done


def shards(state, kernel, bias, innovations, interp, cells, counts):
    group, rows, width = state.shape
    parts, slabs = lax.axis_size("chan"), lax.axis_size("lat")
    wide = padded_width(width)
    total = kernel.shape[2]
    chan_place = lax.axis_index("chan").reshape(1)
    forward_weights = kernel.reshape(3, 3 * total, total)
    backward_weights = jnp.transpose(kernel[::-1, ::-1], (0, 1, 3, 2)).reshape(3, 3 * total, total)

    pieces = split_rows(chan_place, state, parts, wide)

    def send_obs(ahead):
        used, rows_of, cells_of = lax.optimization_barrier((counts, interp, cells, ahead))[:3]
        interp_rows = jnp.transpose(rows_of[:, 0], (1, 0, 2)).astype(jnp.float32)
        packed = pack_obs(used, innovations[:, 0], interp_rows, cells_of[0][:, None, :], width)
        return lax.all_to_all(packed, "lat", split_axis=0, concat_axis=0, tiled=True)

    obs = send_obs(pieces[0])
    mixed, one = mix(
        chan_place, forward_weights, pieces, parts, (obs,),
        lambda ahead: sort_obs(after(obs, ahead), 0, slabs // 2),
    )
    two = sort_obs(after(obs, mixed[-parts]), slabs // 2, slabs // 2)
    grads, departures = observe(chan_place, one, two, bias[:, None], mixed, parts, width)
    grad_pieces, (unsorted,) = mix(
        chan_place, backward_weights, grads, parts, (),
        lambda ahead: [unsort_obs(after(departures, ahead), one[1], two[1], slabs)],
    )
    returned = lax.all_to_all(
        after(unsorted, *grad_pieces[:1 - parts]), "lat", split_axis=0, concat_axis=0, tiled=True
    )
    departures_out = unpack_obs(returned).reshape(innovations.shape)
    grad_state = join_rows(chan_place, grad_pieces, parts, width)
    return grad_state, departures_out


def solution(mesh):
    return jax.shard_map(
        shards,
        mesh=mesh,
        in_specs=(
            P("chan", "lat", None),
            P(),
            P("chan"),
            P("chan", "lat", None, None),
            P(None, "lat", None, None),
            P("lat", None, None),
            P("lat", None),
        ),
        out_specs=(P("chan", "lat", None), P("chan", "lat", None, None)),
        check_vma=False,
    )
```

```python
import functools

import jax
import jax.numpy as jnp
from jax import lax
from jax.experimental import pallas as pl
from jax.experimental.pallas import tpu as pltpu
from jax.sharding import PartitionSpec as P

SPACING = 8
LANES = 128
STEP = 120
TOGETHER = 4
WINDOW = 12
OBS = 256
SIDE = 16
JOIN = 2

VMEM = pl.BlockSpec(memory_space=pltpu.VMEM)
SMEM = pl.BlockSpec(memory_space=pltpu.SMEM)
CONV = pl.CostEstimate(flops=7 * 10**9, bytes_accessed=1000, transcendentals=0)
SMALL = pl.CostEstimate(flops=1000, bytes_accessed=1000, transcendentals=0)
PARAMS = pltpu.CompilerParams(vmem_limit_bytes=56 * 1024 * 1024)


def padded_width(width):
    return -(-(width + 3 * SPACING) // LANES) * LANES


def lane_iota(shape):
    return lax.broadcasted_iota(jnp.int32, shape, len(shape) - 1)


def wrapped_tail(first, tail, rem):
    lane = lane_iota(tail.shape)
    head = pltpu.roll(first, rem, 1)
    end = pltpu.roll(tail, LANES - rem, 1)
    out = jnp.where(lane < rem, tail, jnp.where(lane < rem + 2 * SPACING, head, 0.0))
    return jnp.where(lane >= LANES - SPACING, end, out)


def split_rows_kernel(parts, place_ref, state_ref, *refs):
    outs, rows_ref = refs[:-1], refs[-1]
    group, rows, width = state_ref.shape
    wide = outs[0].shape[1]
    main = width // LANES * LANES
    rem = width - main
    tiles = wide // LANES
    for tile in range(tiles):
        size = min(LANES, width - tile * LANES)
        part = state_ref[:, :, tile * LANES:tile * LANES + size].astype(jnp.float32)
        rows_ref[tile, :, :size] = part.reshape(group * rows, size)
    for number in range(rows):
        if number < parts:
            out, row = outs[number], place_ref[0] ^ number
        else:
            out, row = outs[parts - 1 + number // parts].at[number % parts * group:(number % parts + 1) * group], number
        strips = [rows_ref[tile, pl.ds(row, group, stride=rows), :] for tile in range(tiles)]
        for tile in range(tiles - 1):
            out[:, tile * LANES:(tile + 1) * LANES] = strips[tile].astype(jnp.bfloat16)
        out[:, main:] = wrapped_tail(strips[0], strips[-1], rem).astype(jnp.bfloat16)


def split_rows(place, state, parts, wide):
    group, rows, width = state.shape
    later = rows // parts - 1
    results = pl.pallas_call(
        functools.partial(split_rows_kernel, parts),
        out_shape=[jax.ShapeDtypeStruct((group, wide), jnp.bfloat16)] * parts
        + [jax.ShapeDtypeStruct((parts * group, wide), jnp.bfloat16)] * later,
        in_specs=[SMEM, VMEM],
        out_specs=[VMEM] * (parts + later),
        scratch_shapes=[pltpu.VMEM((wide // LANES, group * rows, LANES), jnp.float32)],
        compiler_params=PARAMS,
        cost_estimate=SMALL,
        name="split_rows",
    )(place, state)
    return [results[:parts], *results[parts:]]


def join_rows_kernel(parts, place_ref, *refs):
    pieces, out_ref, rows_ref = refs[:-2], refs[-2], refs[-1]
    group, rows, width = out_ref.shape
    for number in range(rows):
        turn, k = divmod(number, parts)
        if turn and turn == rows // parts - 1:
            piece, row = pieces[turn + k], turn * parts + (place_ref[0] ^ k)
        else:
            piece, row = pieces[turn].at[k * group:(k + 1) * group], number
        for tile in range(rows_ref.shape[0]):
            part = piece[:, tile * LANES:(tile + 1) * LANES].astype(jnp.float32)
            rows_ref[tile, pl.ds(row, group, stride=rows), :] = part
    for tile in range(rows_ref.shape[0]):
        size = min(LANES, width - tile * LANES)
        part = rows_ref[tile, :, :size].reshape(group, rows, size)
        out_ref[:, :, tile * LANES:tile * LANES + size] = part.astype(jnp.bfloat16)


def join_rows(place, blocks, parts, width):
    pieces = [piece for block in blocks for piece in (block if isinstance(block, list) else [block])]
    group, wide = blocks[0].shape[0] // parts, blocks[0].shape[1]
    rows = parts * len(blocks)
    return pl.pallas_call(
        functools.partial(join_rows_kernel, parts),
        out_shape=jax.ShapeDtypeStruct((group, rows, width), jnp.bfloat16),
        in_specs=[SMEM] + [VMEM] * len(pieces),
        out_specs=VMEM,
        scratch_shapes=[pltpu.VMEM((wide // LANES, group * rows, LANES), jnp.float32)],
        compiler_params=PARAMS,
        cost_estimate=SMALL,
        name="join_rows",
    )(place, *pieces)


def assemble_kernel(place_ref, *refs):
    pieces, out_ref = refs[:-1], refs[-1]
    group = pieces[0].shape[0]
    for k, piece in enumerate(pieces):
        start = pl.multiple_of((place_ref[0] ^ k) * group, group)
        out_ref[pl.ds(start, group), :] = piece[...]


def assemble(place, pieces):
    group, wide = pieces[0].shape
    return pl.pallas_call(
        assemble_kernel,
        out_shape=jax.ShapeDtypeStruct((group * len(pieces), wide), jnp.bfloat16),
        in_specs=[SMEM] + [VMEM] * len(pieces),
        out_specs=VMEM,
        compiler_params=PARAMS,
        cost_estimate=SMALL,
        name="assemble",
    )(place, *pieces)


def conv_kernel(place_ref, weights_ref, below_ref, here_ref, above_ref, *refs):
    outs, sums_ref = refs[:-1], refs[-1]
    total, wide = here_ref.shape
    columns = 4 * LANES
    share = total // max(len(outs), 4)

    @pl.loop(0, wide // columns)
    def _(tile):
        at = pl.ds(pl.multiple_of(tile * columns, columns), columns)
        part = jnp.dot(weights_ref[1], here_ref[:, at], preferred_element_type=jnp.float32)
        part += jnp.dot(weights_ref[0], below_ref[:, at], preferred_element_type=jnp.float32)
        part += jnp.dot(weights_ref[2], above_ref[:, at], preferred_element_type=jnp.float32)
        sums_ref[:, at] = part

    for number in range(total // share):
        if len(outs) > 1:
            out, start = outs[number], pl.multiple_of((place_ref[0] ^ number) * share, share)
        else:
            out, start = outs[0].at[number * share:(number + 1) * share], number * share
        left = sums_ref[pl.ds(start, share), :]
        middle = sums_ref[pl.ds(start + total, share), :]
        right = sums_ref[pl.ds(start + 2 * total, share), :]
        mixed = middle + pltpu.roll(left, SPACING, 1) + pltpu.roll(right, wide - SPACING, 1)
        out[...] = mixed.astype(jnp.bfloat16)


def conv(place, weights, below, here, above, parts):
    total, wide = here.shape
    results = pl.pallas_call(
        conv_kernel,
        out_shape=[jax.ShapeDtypeStruct((total // parts, wide), jnp.bfloat16)] * parts,
        in_specs=[SMEM] + [VMEM] * 4,
        out_specs=[VMEM] * parts,
        scratch_shapes=[pltpu.VMEM((3 * total, wide), jnp.float32)],
        compiler_params=PARAMS,
        cost_estimate=CONV,
        name="conv",
    )(place, weights, below, here, above)
    return results if parts > 1 else results[0]


def pack_obs_kernel(width, counts_ref, values_ref, weights_ref, cells_ref, out_ref, tiles_ref):
    slabs, depth, slots = out_ref.shape
    group = depth - SIDE
    blocks = -(-width // STEP)
    for tile in range(slots // LANES):
        tiles_ref[tile] = values_ref[:, tile * LANES:(tile + 1) * LANES]
    for slab in range(slabs):
        used = lane_iota((1, slots)) < counts_ref[0, slab]
        values = jnp.concatenate(
            [tiles_ref[tile, pl.ds(slab, group, stride=slabs), :] for tile in range(slots // LANES)], axis=1
        )
        out_ref[slab, :group, :] = jnp.where(used, values, 0.0).astype(jnp.bfloat16)
        weights = jnp.where(used, weights_ref[slab], 0.0)
        local = (cells_ref[slab] - slab * (SPACING * width)).astype(jnp.float32)
        row = jnp.clip(jnp.floor((local + 0.5) * (1.0 / width)), 0.0, SPACING - 2.0)
        column = local - row * width
        block = jnp.clip(jnp.floor((column + 0.5) * (1.0 / STEP)), 0.0, blocks - 1.0)
        side = jnp.concatenate(
            [weights, row * blocks + block, column - block * STEP, jnp.zeros((SIDE - 6, slots), jnp.float32)],
            axis=0,
        )
        out_ref[slab, group:, :] = side.astype(jnp.bfloat16)


def pack_obs(counts, values, weights, cells, width):
    group, slabs, slots = values.shape
    return pl.pallas_call(
        functools.partial(pack_obs_kernel, width),
        out_shape=jax.ShapeDtypeStruct((slabs, group + SIDE, slots), jnp.bfloat16),
        in_specs=[SMEM, VMEM, VMEM, VMEM],
        out_specs=VMEM,
        scratch_shapes=[pltpu.VMEM((slots // LANES, group * slabs, LANES), jnp.float32)],
        compiler_params=PARAMS,
        cost_estimate=SMALL,
        name="pack_obs",
    )(counts, values.reshape(group * slabs, slots), weights, cells)


def sort_obs_kernel(begin, obs_ref, sorted_ref, rank_ref, first_ref, last_ref, joined_ref, column_ref):
    sets, depth, size = sorted_ref.shape
    group = depth - SIDE
    each = obs_ref.shape[2]
    for s in range(sets):
        for i in range(size // each):
            joined_ref[:, i * each:(i + 1) * each] = obs_ref[begin + s * (size // each) + i]
        which = joined_ref[group:, :].astype(jnp.float32)[4:5]
        key = which * size + lane_iota((1, size)).astype(jnp.float32)
        column_ref[...] = jnp.transpose(jnp.broadcast_to(key, (LANES, size)))
        ranks = []
        for tile in range(size // LANES):
            below = jnp.where(column_ref[...] < key[:, tile * LANES:(tile + 1) * LANES], 1.0, 0.0)
            ranks.append(jnp.sum(below, axis=0, keepdims=True))
        rank = jnp.concatenate(ranks, axis=1)
        rank_ref[s] = rank.astype(jnp.int32)
        column_ref[...] = jnp.transpose(jnp.broadcast_to(rank, (LANES, size)))

        @pl.loop(0, size // OBS)
        def _(tile):
            start = pl.multiple_of(tile * OBS, OBS)
            chosen = []
            for i in range(OBS // LANES):
                order = (lane_iota((1, LANES)) + (start + i * LANES)).astype(jnp.float32)
                chosen.append(jnp.where(column_ref[...] == order, 1.0, 0.0).astype(jnp.bfloat16))
            taken = jnp.dot(
                joined_ref[...], jnp.concatenate(chosen, axis=1), preferred_element_type=jnp.float32
            )
            sorted_ref[s, :, pl.ds(start, OBS)] = taken.astype(jnp.bfloat16)
            which = taken[group + 4:group + 5]
            first_ref[s * (size // OBS) + tile] = jnp.min(which).astype(jnp.int32)
            last_ref[s * (size // OBS) + tile] = jnp.max(which).astype(jnp.int32)


def sort_obs(obs, begin, slabs):
    depth, slots = obs.shape[1:]
    size = slots * JOIN
    sets = slabs // JOIN
    return pl.pallas_call(
        functools.partial(sort_obs_kernel, begin),
        out_shape=[
            jax.ShapeDtypeStruct((sets, depth, size), jnp.bfloat16),
            jax.ShapeDtypeStruct((sets, 1, size), jnp.int32),
            jax.ShapeDtypeStruct((sets * size // OBS,), jnp.int32),
            jax.ShapeDtypeStruct((sets * size // OBS,), jnp.int32),
        ],
        in_specs=[VMEM],
        out_specs=[VMEM, VMEM, SMEM, SMEM],
        scratch_shapes=[pltpu.VMEM((depth, size), jnp.bfloat16), pltpu.VMEM((size, LANES), jnp.float32)],
        compiler_params=PARAMS,
        cost_estimate=SMALL,
        name="sort_obs",
    )(obs)


def unsort_obs_kernel(sorted_ref, one_ref, two_ref, out_ref):
    sets, group, size = sorted_ref.shape
    each = out_ref.shape[2]
    for s in range(sets):
        @pl.loop(0, size // OBS)
        def _(tile):
            start = pl.multiple_of(tile * OBS, OBS)
            rank = (one_ref if s < sets // 2 else two_ref)[s % (sets // 2), :, pl.ds(start, OBS)]
            chosen = jnp.where(lax.broadcasted_iota(jnp.int32, (size, OBS), 0) == rank, 1.0, 0.0)
            taken = jnp.dot(sorted_ref[s], chosen.astype(jnp.bfloat16), preferred_element_type=jnp.float32)
            slab = s * (size // each) + tile // (each // OBS)
            at = pl.ds(pl.multiple_of(tile % (each // OBS) * OBS, OBS), OBS)
            out_ref[slab, :, at] = taken.astype(jnp.bfloat16)


def unsort_obs(values, one, two, slabs):
    sets, group, size = values.shape
    return pl.pallas_call(
        unsort_obs_kernel,
        out_shape=jax.ShapeDtypeStruct((slabs, group, sets * size // slabs), jnp.bfloat16),
        in_specs=[VMEM] * 3,
        out_specs=VMEM,
        compiler_params=PARAMS,
        cost_estimate=SMALL,
        name="unsort_obs",
    )(values, one, two)


def unpack_obs_kernel(values_ref, out_ref, tiles_ref):
    slabs, group, slots = values_ref.shape
    for slab in range(slabs):
        for tile in range(slots // LANES):
            part = values_ref[slab, :, tile * LANES:(tile + 1) * LANES].astype(jnp.float32)
            tiles_ref[tile, pl.ds(slab, group, stride=slabs), :] = part
    for tile in range(slots // LANES):
        out_ref[:, tile * LANES:(tile + 1) * LANES] = tiles_ref[tile]


def unpack_obs(values):
    slabs, group, slots = values.shape
    return pl.pallas_call(
        unpack_obs_kernel,
        out_shape=jax.ShapeDtypeStruct((group * slabs, slots), jnp.float32),
        in_specs=[VMEM],
        out_specs=VMEM,
        scratch_shapes=[pltpu.VMEM((slots // LANES, group * slabs, LANES), jnp.float32)],
        compiler_params=PARAMS,
        cost_estimate=SMALL,
        name="unpack_obs",
    )(values)


def activate_kernel(parts, width, place_ref, bias_ref, *refs):
    pieces, table_ref, slope_ref = refs[:-2], refs[-2], refs[-1]
    blocks = -(-width // STEP)
    group, wide = slope_ref.shape[0] // parts, slope_ref.shape[1]
    lane = lane_iota((group, LANES))
    for k in range(parts):
        row = place_ref[0] ^ k if len(pieces) > 1 else k
        piece = pieces[k] if len(pieces) > 1 else pieces[0].at[k * group:(k + 1) * group]
        rows_at = pl.ds(pl.multiple_of(row * group, group), group)
        hidden = []
        for tile in range(wide // LANES):
            at = slice(tile * LANES, (tile + 1) * LANES)
            value = piece[:, at].astype(jnp.float32) + bias_ref[...]
            half = 0.5 * (1.0 + lax.erf(value * 0.7071067811865476))
            hidden.append(value * half)
            slope_ref[rows_at, at] = half + value * jnp.exp(-0.5 * value * value) * 0.3989422804014327
        for j in range(blocks):
            tile, shift = divmod(j * STEP, LANES)
            block = hidden[tile]
            if shift:
                block = jnp.where(
                    lane < LANES - shift,
                    pltpu.roll(block, LANES - shift, 1),
                    pltpu.roll(hidden[tile + 1], LANES - shift, 1),
                )
            start = pl.multiple_of((row * blocks + j) * group, group)
            table_ref[pl.ds(start, group), :] = block.astype(jnp.bfloat16)


def activate(place, bias, block, parts, width):
    pieces = block if isinstance(block, list) else [block]
    group, wide = bias.shape[0], pieces[0].shape[1]
    blocks = -(-width // STEP)
    return pl.pallas_call(
        functools.partial(activate_kernel, parts, width),
        out_shape=[
            jax.ShapeDtypeStruct((parts * blocks * group, LANES), jnp.bfloat16),
            jax.ShapeDtypeStruct((parts * group, wide), jnp.float32),
        ],
        in_specs=[SMEM] + [VMEM] * (1 + len(pieces)),
        out_specs=[VMEM] * 2,
        compiler_params=PARAMS,
        cost_estimate=SMALL,
        name="activate",
    )(place, bias, *pieces)


def observe_kernel(parts, turns, width, place_ref, *refs):
    rows = parts * turns
    firsts, lasts, halves = refs[0:2], refs[2:4], refs[4:6]
    tables, slopes, refs = refs[6:6 + turns], refs[6 + turns:6 + 2 * turns], refs[6 + 2 * turns:]
    pieces, grads, refs = refs[:parts], refs[parts:parts + turns - 1], refs[parts + turns - 1:]
    departure_ref, table_ref, found_ref, obs_ref, spread_ref, first_ref, arrival = refs
    grads = [first_ref, *grads]
    group, wide = slopes[0].shape[0] // parts, slopes[0].shape[1]
    size = obs_ref.shape[2]
    sets = obs_ref.shape[0] // 2
    blocks = -(-width // STEP)
    tiles = wide // LANES
    rem = width % LANES
    last = width // LANES
    lane = lane_iota((group, LANES))
    slab = blocks * group
    high = WINDOW * group

    copies = [
        pltpu.make_async_copy(half, obs_ref.at[pl.ds(i * sets, sets)], arrival.at[i])
        for i, half in enumerate(halves)
    ]
    for i, table in enumerate(tables):
        for lanes in range(2):
            start = (i * parts + 1 - lanes) * slab
            target = table_ref.at[pl.ds(start, parts * slab), pl.ds(lanes * LANES, LANES)]
            copies.append(pltpu.make_async_copy(table, target, arrival.at[2 + 2 * i + lanes]))
    for copy in copies:
        copy.start()
    for copy in copies:
        copy.wait()

    count = firsts[0].shape[0]
    lo_iota = lax.broadcasted_iota(jnp.int32, (LANES, OBS), 0)
    share = found_ref.shape[0] // (2 * count // TOGETHER)

    def find(number):
        s = number // (size // OBS)
        at = pl.ds(pl.multiple_of(number % (size // OBS) * OBS, OBS), OBS)
        side = obs_ref[s, group:, at].astype(jnp.float32)
        whole = jnp.broadcast_to(side[4:5].astype(jnp.int32), (8, OBS))
        here, there = jnp.minimum(number, count - 1), jnp.maximum(number - count, 0)
        lowest = jnp.where(number < count, firsts[0][here], firsts[1][there])
        highest = jnp.where(number < count, lasts[0][here], lasts[1][there])
        lowest = jnp.clip(lowest, 0, (rows - 1) * blocks - 1)
        highest = jnp.clip(highest, lowest, (rows - 1) * blocks - 1)
        return s, at, side, whole, lowest, (highest - lowest) // WINDOW + 1

    @pl.loop(0, 2 * count // TOGETHER)
    def _(batch):
        start = pl.multiple_of(batch * share, share)
        found_ref[pl.ds(start, share), :] = jnp.zeros((share, 2 * LANES), jnp.float32)
        items, spreads = [find(batch * TOGETHER + i) for i in range(TOGETHER)], []
        for i, (_, _, side, _, _, _) in enumerate(items):
            low = side[5:6].astype(jnp.int32)
            first, second = lo_iota == low, lo_iota == low + 1
            spread = jnp.concatenate(
                [
                    jnp.where(first, side[0:1], jnp.where(second, side[1:2], 0.0)),
                    jnp.where(first, side[2:3], jnp.where(second, side[3:4], 0.0)),
                ],
                axis=0,
            ).astype(jnp.bfloat16)
            spread_ref[batch * TOGETHER + i] = spread
            spreads.append(spread)

        def gather(item, spread, window, model):
            _, _, _, whole, lowest, _ = item
            base = lowest + window * WINDOW
            at = pl.ds(pl.multiple_of((base + blocks) * group, group), high)
            part = jnp.dot(table_ref[at, :], spread, preferred_element_type=jnp.float32)
            for i in range(WINDOW):
                block = part[i * group:(i + 1) * group].reshape(group // 8, 8, OBS)
                model = jnp.where((whole == base + i)[None], block, model)
            return model

        zero = jnp.zeros((group // 8, 8, OBS), jnp.float32)
        models = [gather(item, spread, 0, zero) for item, spread in zip(items, spreads)]

        def more(window, models):
            return [
                gather(item, spread_ref[batch * TOGETHER + i], jnp.minimum(window, item[-1] - 1), model)
                for i, (item, model) in enumerate(zip(items, models))
            ]

        models = lax.fori_loop(1, functools.reduce(jnp.maximum, [item[-1] for item in items]), more, models)
        for (s, at, _, _, _, _), model in zip(items, models):
            departure = model.reshape(group, OBS) - obs_ref[s, :group, at].astype(jnp.float32)
            departure_ref[s, :, at] = departure.astype(jnp.bfloat16)

    @pl.loop(0, 2 * count // TOGETHER)
    def _(batch):
        items = [find(batch * TOGETHER + i) for i in range(TOGETHER)]

        def scatter(i, window):
            s, at, _, whole, lowest, _ = items[i]
            departure = departure_ref[s, :, at].astype(jnp.float32).reshape(group // 8, 8, OBS)
            base = lowest + window * WINDOW
            chosen = [
                jnp.where((whole == base + i)[None], departure, 0.0).reshape(group, OBS) for i in range(WINDOW)
            ]
            rows_at = pl.ds(pl.multiple_of(base * group, group), high)
            found_ref[rows_at, :] += lax.dot_general(
                jnp.concatenate(chosen, axis=0).astype(jnp.bfloat16),
                spread_ref[batch * TOGETHER + i],
                (((1,), (1,)), ((), ())),
                preferred_element_type=jnp.float32,
            )

        for i in range(TOGETHER):
            scatter(i, 0)
        for i in range(TOGETHER):
            pl.loop(1, items[i][-1])(functools.partial(scatter, i))

    for row in range(rows):
        out, slope = [ref.at[row % parts * group:(row % parts + 1) * group] for ref in (grads[row // parts], slopes[row // parts])]
        sums = [jnp.zeros((group, LANES), jnp.float32) for _ in range(tiles)]
        for j in range(blocks):
            tile, shift = divmod(j * STEP, LANES)
            block = jnp.zeros((group, LANES), jnp.float32)
            if row < rows - 1:
                start = (row * blocks + j) * group
                block += found_ref[start:start + group, :LANES]
            if row > 0:
                start = ((row - 1) * blocks + j) * group
                block += found_ref[start:start + group, LANES:]
            if shift:
                block = pltpu.roll(block, shift, 1)
                sums[tile] += jnp.where(lane >= shift, block, 0.0)
                sums[tile + 1] += jnp.where(lane < shift, block, 0.0)
            else:
                sums[tile] += block
        sums[0] += jnp.where(lane == 0, pltpu.roll(sums[last], LANES - rem, 1), 0.0)
        for tile in range(tiles):
            at = slice(tile * LANES, (tile + 1) * LANES)
            sums[tile] *= slope[:, at]
            if tile < last:
                out[:, at] = sums[tile].astype(jnp.bfloat16)
        out[:, last * LANES:] = wrapped_tail(sums[0], sums[last], rem).astype(jnp.bfloat16)
    for k, piece in enumerate(pieces):
        piece[...] = first_ref[pl.ds(pl.multiple_of((place_ref[0] ^ k) * group, group), group), :]


def observe(place, one, two, tables, slopes, parts, width):
    group, wide = slopes[0].shape[0] // parts, slopes[0].shape[1]
    turns = len(slopes)
    rows = parts * turns
    blocks = -(-width // STEP)
    sets, depth, size = 2 * one[0].shape[0], one[0].shape[1], one[0].shape[2]
    numbers = sets * size // OBS
    found = -(-((rows - 1) * blocks + WINDOW) * group * TOGETHER // numbers // 8) * 8 * numbers // TOGETHER
    results = pl.pallas_call(
        functools.partial(observe_kernel, parts, turns, width),
        out_shape=[jax.ShapeDtypeStruct((group, wide), jnp.bfloat16)] * parts
        + [jax.ShapeDtypeStruct((parts * group, wide), jnp.bfloat16)] * (turns - 1)
        + [jax.ShapeDtypeStruct((sets, group, size), jnp.bfloat16)],
        in_specs=[SMEM] * 5 + [pl.BlockSpec(memory_space=pl.ANY)] * (2 + turns) + [VMEM] * turns,
        out_specs=[VMEM] * (parts + turns),
        scratch_shapes=[
            pltpu.VMEM(((rows + 1) * blocks * group, 2 * LANES), jnp.bfloat16),
            pltpu.VMEM((found, 2 * LANES), jnp.float32),
            pltpu.VMEM((sets, depth, size), jnp.bfloat16),
            pltpu.VMEM((numbers, 2 * LANES, OBS), jnp.bfloat16),
            pltpu.VMEM((parts * group, wide), jnp.bfloat16),
            pltpu.SemaphoreType.DMA((2 + 2 * turns,)),
        ],
        compiler_params=PARAMS,
        cost_estimate=SMALL,
        name="observe",
    )(place, one[2], two[2], one[3], two[3], one[0], two[0], *tables, *slopes)
    return [results[:parts], *results[parts:-1]], results[-1]


def after(value, *others):
    return lax.optimization_barrier((value, *others))[0]


def turn_over(block, axis):
    return lax.all_to_all(block, axis, split_axis=0, concat_axis=0, tiled=True)


def swap(pieces):
    count = lax.axis_size("chan")
    return [pieces[0]] + [
        lax.ppermute(pieces[k], "chan", [(i, i ^ k) for i in range(count)]) for k in range(1, count)
    ]


def mix(place, weights, blocks, ahead=(), between=None):
    count, turns = lax.axis_size("lat"), len(blocks)
    forward = [(i, i + 1) for i in range(count - 1)]
    backward = [(i + 1, i) for i in range(count - 1)]
    pieces = swap(blocks[0])
    heres = [after(assemble(place, pieces), *ahead)]
    for block in blocks[1:]:
        heres.append(turn_over(after(block, *pieces[1:]), "chan"))
    done = () if between is None else between(heres[0])
    if turns > 1:
        heres[1] = after(heres[1], *done)
    results, mixed = [], ()
    for turn in range(turns):
        here = heres[turn]
        halos = [lax.ppermute(here, "lat", forward), lax.ppermute(here, "lat", backward)]
        ready = after(here, *mixed, *heres[turn + 1:turn + 2], *done)
        split = lax.axis_size("chan") if turn and turn == turns - 1 else 1
        mixed = conv(place, weights, halos[0], ready, halos[1], split)
        if split > 1:
            mixed = list(mixed)
            results.append(swap(mixed))
        else:
            results.append(turn_over(after(mixed, *results[-1:]), "chan"))
            mixed = [mixed]
    return results, done, mixed[0]


def shards(state, kernel, bias, innovations, interp, cells, counts):
    rows, width = state.shape[1:]
    parts, slabs = lax.axis_size("chan"), lax.axis_size("lat")
    total = kernel.shape[2]
    place = lax.axis_index("chan").reshape(1)
    forward_weights = kernel.reshape(3, 3 * total, total)
    backward_weights = jnp.transpose(kernel[::-1, ::-1], (0, 1, 3, 2)).reshape(3, 3 * total, total)

    blocks = split_rows(place, state, parts, padded_width(width))

    used, rows_of, cells_of = lax.optimization_barrier((counts, interp, cells, blocks[0][0]))[:3]
    interp_rows = jnp.transpose(rows_of[:, 0], (1, 0, 2)).astype(jnp.float32)
    packed = pack_obs(used, innovations[:, 0], interp_rows, cells_of[0][:, None, :], width)
    obs = turn_over(packed, "lat")
    mixed, one, last = mix(
        place, forward_weights, blocks, (obs,), lambda ahead: sort_obs(after(obs, ahead), 0, slabs // 2)
    )
    two = sort_obs(after(obs, last), slabs // 2, slabs // 2)

    tables, slopes = [], []
    for block in mixed:
        table, slope = activate(after(place, *tables), bias[:, None], block, parts, width)
        tables.append(table)
        slopes.append(slope)
    grads, departures = observe(place, one, two, tables, slopes, parts, width)
    grad_blocks, (unsorted,), last = mix(
        place, backward_weights, grads, (),
        lambda ahead: [unsort_obs(after(departures, ahead), one[1], two[1], slabs)],
    )
    departures_out = unpack_obs(turn_over(after(unsorted, last, *grad_blocks[:-1]), "lat"))
    grad_state = join_rows(after(place, departures_out), grad_blocks, parts, width)
    return grad_state, departures_out.reshape(innovations.shape)


def solution(mesh):
    return jax.shard_map(
        shards,
        mesh=mesh,
        in_specs=(
            P("chan", "lat", None),
            P(),
            P("chan"),
            P("chan", "lat", None, None),
            P(None, "lat", None, None),
            P("lat", None, None),
            P("lat", None),
        ),
        out_specs=(P("chan", "lat", None), P("chan", "lat", None, None)),
        check_vma=False,
    )
```

```python
import functools

import jax
import jax.numpy as jnp
from jax import lax
from jax.experimental import pallas as pl
from jax.experimental.pallas import tpu as pltpu
from jax.sharding import PartitionSpec as P

SPACING = 8
LANES = 128
STEP = 120
TOGETHER = 4
WINDOW = 12
OBS = 256
SIDE = 16
JOIN = 2

VMEM = pl.BlockSpec(memory_space=pltpu.VMEM)
SMEM = pl.BlockSpec(memory_space=pltpu.SMEM)
CONV = pl.CostEstimate(flops=7 * 10**9, bytes_accessed=1000, transcendentals=0)
SMALL = pl.CostEstimate(flops=1000, bytes_accessed=1000, transcendentals=0)
PARAMS = pltpu.CompilerParams(vmem_limit_bytes=56 * 1024 * 1024)


def padded_width(width):
    return -(-(width + 3 * SPACING) // LANES) * LANES


def lane_iota(shape):
    return lax.broadcasted_iota(jnp.int32, shape, len(shape) - 1)


def wrapped_tail(first, tail, rem):
    lane = lane_iota(tail.shape)
    head = pltpu.roll(first, rem, 1)
    end = pltpu.roll(tail, LANES - rem, 1)
    out = jnp.where(lane < rem, tail, jnp.where(lane < rem + 2 * SPACING, head, 0.0))
    return jnp.where(lane >= LANES - SPACING, end, out)


def split_rows_kernel(parts, place_ref, state_ref, *refs):
    outs, rows_ref = refs[:-1], refs[-1]
    group, rows, width = state_ref.shape
    wide = outs[0].shape[1]
    main = width // LANES * LANES
    rem = width - main
    tiles = wide // LANES
    for tile in range(tiles):
        size = min(LANES, width - tile * LANES)
        part = state_ref[:, :, tile * LANES:tile * LANES + size].astype(jnp.float32)
        rows_ref[tile, :, :size] = part.reshape(group * rows, size)
    for number in range(rows):
        if number < parts:
            out, row = outs[number], place_ref[0] ^ number
        else:
            out, row = outs[parts - 1 + number // parts].at[number % parts * group:(number % parts + 1) * group], number
        strips = [rows_ref[tile, pl.ds(row, group, stride=rows), :] for tile in range(tiles)]
        for tile in range(tiles - 1):
            out[:, tile * LANES:(tile + 1) * LANES] = strips[tile].astype(jnp.bfloat16)
        out[:, main:] = wrapped_tail(strips[0], strips[-1], rem).astype(jnp.bfloat16)


def split_rows(place, state, parts, wide):
    group, rows, width = state.shape
    later = rows // parts - 1
    results = pl.pallas_call(
        functools.partial(split_rows_kernel, parts),
        out_shape=[jax.ShapeDtypeStruct((group, wide), jnp.bfloat16)] * parts
        + [jax.ShapeDtypeStruct((parts * group, wide), jnp.bfloat16)] * later,
        in_specs=[SMEM, VMEM],
        out_specs=[VMEM] * (parts + later),
        scratch_shapes=[pltpu.VMEM((wide // LANES, group * rows, LANES), jnp.float32)],
        compiler_params=PARAMS,
        cost_estimate=SMALL,
        name="split_rows",
    )(place, state)
    return [results[:parts], *results[parts:]]


def join_rows_kernel(parts, place_ref, *refs):
    pieces, out_ref, rows_ref = refs[:-2], refs[-2], refs[-1]
    group, rows, width = out_ref.shape
    for number in range(rows):
        turn, k = divmod(number, parts)
        if turn and turn == rows // parts - 1:
            piece, row = pieces[turn + k], turn * parts + (place_ref[0] ^ k)
        else:
            piece, row = pieces[turn].at[k * group:(k + 1) * group], number
        for tile in range(rows_ref.shape[0]):
            part = piece[:, tile * LANES:(tile + 1) * LANES].astype(jnp.float32)
            rows_ref[tile, pl.ds(row, group, stride=rows), :] = part
    for tile in range(rows_ref.shape[0]):
        size = min(LANES, width - tile * LANES)
        part = rows_ref[tile, :, :size].reshape(group, rows, size)
        out_ref[:, :, tile * LANES:tile * LANES + size] = part.astype(jnp.bfloat16)


def join_rows(place, blocks, parts, width):
    pieces = [piece for block in blocks for piece in (block if isinstance(block, list) else [block])]
    group, wide = blocks[0].shape[0] // parts, blocks[0].shape[1]
    rows = parts * len(blocks)
    return pl.pallas_call(
        functools.partial(join_rows_kernel, parts),
        out_shape=jax.ShapeDtypeStruct((group, rows, width), jnp.bfloat16),
        in_specs=[SMEM] + [VMEM] * len(pieces),
        out_specs=VMEM,
        scratch_shapes=[pltpu.VMEM((wide // LANES, group * rows, LANES), jnp.float32)],
        compiler_params=PARAMS,
        cost_estimate=SMALL,
        name="join_rows",
    )(place, *pieces)


def assemble_kernel(place_ref, *refs):
    pieces, out_ref = refs[:-1], refs[-1]
    group = pieces[0].shape[0]
    for k, piece in enumerate(pieces):
        start = pl.multiple_of((place_ref[0] ^ k) * group, group)
        out_ref[pl.ds(start, group), :] = piece[...]


def assemble(place, pieces):
    group, wide = pieces[0].shape
    return pl.pallas_call(
        assemble_kernel,
        out_shape=jax.ShapeDtypeStruct((group * len(pieces), wide), jnp.bfloat16),
        in_specs=[SMEM] + [VMEM] * len(pieces),
        out_specs=VMEM,
        compiler_params=PARAMS,
        cost_estimate=SMALL,
        name="assemble",
    )(place, *pieces)


def conv_kernel(place_ref, weights_ref, below_ref, here_ref, above_ref, *refs):
    outs, sums_ref = refs[:-1], refs[-1]
    total, wide = here_ref.shape
    columns = 4 * LANES
    share = total // max(len(outs), 4)

    @pl.loop(0, wide // columns)
    def _(tile):
        at = pl.ds(pl.multiple_of(tile * columns, columns), columns)
        part = jnp.dot(weights_ref[1], here_ref[:, at], preferred_element_type=jnp.float32)
        part += jnp.dot(weights_ref[0], below_ref[:, at], preferred_element_type=jnp.float32)
        part += jnp.dot(weights_ref[2], above_ref[:, at], preferred_element_type=jnp.float32)
        sums_ref[:, at] = part

    for number in range(total // share):
        if len(outs) > 1:
            out, start = outs[number], pl.multiple_of((place_ref[0] ^ number) * share, share)
        else:
            out, start = outs[0].at[number * share:(number + 1) * share], number * share
        left = sums_ref[pl.ds(start, share), :]
        middle = sums_ref[pl.ds(start + total, share), :]
        right = sums_ref[pl.ds(start + 2 * total, share), :]
        mixed = middle + pltpu.roll(left, SPACING, 1) + pltpu.roll(right, wide - SPACING, 1)
        out[...] = mixed.astype(jnp.bfloat16)


def conv(place, weights, below, here, above, parts):
    total, wide = here.shape
    results = pl.pallas_call(
        conv_kernel,
        out_shape=[jax.ShapeDtypeStruct((total // parts, wide), jnp.bfloat16)] * parts,
        in_specs=[SMEM] + [VMEM] * 4,
        out_specs=[VMEM] * parts,
        scratch_shapes=[pltpu.VMEM((3 * total, wide), jnp.float32)],
        compiler_params=PARAMS,
        cost_estimate=CONV,
        name="conv",
    )(place, weights, below, here, above)
    return results if parts > 1 else results[0]


def pack_obs_kernel(width, counts_ref, values_ref, weights_ref, cells_ref, out_ref, tiles_ref):
    slabs, depth, slots = out_ref.shape
    group = depth - SIDE
    blocks = -(-width // STEP)
    for tile in range(slots // LANES):
        tiles_ref[tile] = values_ref[:, tile * LANES:(tile + 1) * LANES]
    all_weights = weights_ref[...].astype(jnp.float32)
    for slab in range(slabs):
        used = lane_iota((1, slots)) < counts_ref[0, slab]
        values = jnp.concatenate(
            [tiles_ref[tile, pl.ds(slab, group, stride=slabs), :] for tile in range(slots // LANES)], axis=1
        )
        out_ref[slab, :group, :] = jnp.where(used, values, 0.0).astype(jnp.bfloat16)
        weights = jnp.where(used, all_weights[:, 0, slab, :], 0.0)
        local = (cells_ref[0, slab:slab + 1, :] - slab * (SPACING * width)).astype(jnp.float32)
        row = jnp.clip(jnp.floor((local + 0.5) * (1.0 / width)), 0.0, SPACING - 2.0)
        column = local - row * width
        block = jnp.clip(jnp.floor((column + 0.5) * (1.0 / STEP)), 0.0, blocks - 1.0)
        side = jnp.concatenate(
            [weights, row * blocks + block, column - block * STEP, jnp.zeros((SIDE - 6, slots), jnp.float32)],
            axis=0,
        )
        out_ref[slab, group:, :] = side.astype(jnp.bfloat16)


def pack_obs(counts, values, weights, cells, width):
    group, slabs, slots = values.shape
    return pl.pallas_call(
        functools.partial(pack_obs_kernel, width),
        out_shape=jax.ShapeDtypeStruct((slabs, group + SIDE, slots), jnp.bfloat16),
        in_specs=[SMEM, VMEM, VMEM, VMEM],
        out_specs=VMEM,
        scratch_shapes=[pltpu.VMEM((slots // LANES, group * slabs, LANES), jnp.float32)],
        compiler_params=PARAMS,
        cost_estimate=SMALL,
        name="pack_obs",
    )(counts, values.reshape(group * slabs, slots), weights, cells)


def sort_obs_kernel(begin, place_ref, obs_ref, sorted_ref, rank_ref, first_ref, last_ref, joined_ref, column_ref):
    sets, depth, size = sorted_ref.shape
    group = depth - SIDE
    each = obs_ref.shape[2]
    for s in range(sets):
        for i in range(size // each):
            joined_ref[:, i * each:(i + 1) * each] = obs_ref[place_ref[0] ^ (begin + s * (size // each) + i)]
        which = joined_ref[group:, :].astype(jnp.float32)[4:5]
        key = which * size + lane_iota((1, size)).astype(jnp.float32)
        column_ref[...] = jnp.transpose(jnp.broadcast_to(key, (LANES, size)))
        ranks = []
        for tile in range(size // LANES):
            below = jnp.where(column_ref[...] < key[:, tile * LANES:(tile + 1) * LANES], 1.0, 0.0)
            ranks.append(jnp.sum(below, axis=0, keepdims=True))
        rank = jnp.concatenate(ranks, axis=1)
        rank_ref[s] = rank.astype(jnp.int32)
        column_ref[...] = jnp.transpose(jnp.broadcast_to(rank, (LANES, size)))

        @pl.loop(0, size // OBS)
        def _(tile):
            start = pl.multiple_of(tile * OBS, OBS)
            chosen = []
            for i in range(OBS // LANES):
                order = (lane_iota((1, LANES)) + (start + i * LANES)).astype(jnp.float32)
                chosen.append(jnp.where(column_ref[...] == order, 1.0, 0.0).astype(jnp.bfloat16))
            taken = jnp.dot(
                joined_ref[...], jnp.concatenate(chosen, axis=1), preferred_element_type=jnp.float32
            )
            sorted_ref[s, :, pl.ds(start, OBS)] = taken.astype(jnp.bfloat16)
            which = taken[group + 4:group + 5]
            first_ref[s * (size // OBS) + tile] = jnp.min(which).astype(jnp.int32)
            last_ref[s * (size // OBS) + tile] = jnp.max(which).astype(jnp.int32)


def sort_obs(place, obs, begin, slabs):
    depth, slots = obs.shape[1:]
    size = slots * JOIN
    sets = slabs // JOIN
    return pl.pallas_call(
        functools.partial(sort_obs_kernel, begin),
        out_shape=[
            jax.ShapeDtypeStruct((sets, depth, size), jnp.bfloat16),
            jax.ShapeDtypeStruct((sets, 1, size), jnp.int32),
            jax.ShapeDtypeStruct((sets * size // OBS,), jnp.int32),
            jax.ShapeDtypeStruct((sets * size // OBS,), jnp.int32),
        ],
        in_specs=[SMEM, VMEM],
        out_specs=[VMEM, VMEM, SMEM, SMEM],
        scratch_shapes=[pltpu.VMEM((depth, size), jnp.bfloat16), pltpu.VMEM((size, LANES), jnp.float32)],
        compiler_params=PARAMS,
        cost_estimate=SMALL,
        name="sort_obs",
    )(place, obs)


def unsort_obs_kernel(begin, count, sorted_ref, *refs):
    ranks, outs = refs[:-count], refs[-count:]
    size = sorted_ref.shape[2]
    each = outs[0].shape[1]
    places = [(rank_ref, s) for rank_ref in ranks for s in range(rank_ref.shape[0])]
    for number, out in enumerate(outs):
        s, offset = divmod(number * each, size)

        @pl.loop(0, each // OBS)
        def _(tile):
            start = pl.multiple_of(tile * OBS, OBS)
            rank = places[s][0][places[s][1], :, pl.ds(offset + start, OBS)]
            chosen = jnp.where(lax.broadcasted_iota(jnp.int32, (size, OBS), 0) == rank, 1.0, 0.0)
            taken = jnp.dot(
                sorted_ref[begin + s], chosen.astype(jnp.bfloat16), preferred_element_type=jnp.float32
            )
            out[:, pl.ds(start, OBS)] = taken.astype(jnp.bfloat16)


def unsort_obs(values, begin, ranks):
    group, size = values.shape[1:]
    count = sum(rank.shape[0] for rank in ranks) * JOIN
    return pl.pallas_call(
        functools.partial(unsort_obs_kernel, begin, count),
        out_shape=[jax.ShapeDtypeStruct((group, size // JOIN), jnp.bfloat16)] * count,
        in_specs=[VMEM] * (1 + len(ranks)),
        out_specs=[VMEM] * count,
        compiler_params=PARAMS,
        cost_estimate=SMALL,
        name="unsort_obs",
    )(values, *ranks)


def unpack_obs_kernel(place_ref, *refs):
    pieces, out_ref, tiles_ref = refs[:-2], refs[-2], refs[-1]
    slabs = len(pieces)
    group, slots = pieces[0].shape
    for k, piece in enumerate(pieces):
        slab = place_ref[0] ^ k
        for tile in range(slots // LANES):
            part = piece[:, tile * LANES:(tile + 1) * LANES].astype(jnp.float32)
            tiles_ref[tile, pl.ds(slab, group, stride=slabs), :] = part
    for tile in range(slots // LANES):
        out_ref[:, tile * LANES:(tile + 1) * LANES] = tiles_ref[tile]


def unpack_obs(place, pieces):
    slabs = len(pieces)
    group, slots = pieces[0].shape
    return pl.pallas_call(
        unpack_obs_kernel,
        out_shape=jax.ShapeDtypeStruct((group * slabs, slots), jnp.float32),
        in_specs=[SMEM] + [VMEM] * slabs,
        out_specs=VMEM,
        scratch_shapes=[pltpu.VMEM((slots // LANES, group * slabs, LANES), jnp.float32)],
        compiler_params=PARAMS,
        cost_estimate=SMALL,
        name="unpack_obs",
    )(place, *pieces)


def activate_kernel(parts, width, place_ref, bias_ref, *refs):
    pieces, table_ref, slope_ref = refs[:-2], refs[-2], refs[-1]
    blocks = -(-width // STEP)
    group, wide = slope_ref.shape[0] // parts, slope_ref.shape[1]
    lane = lane_iota((group, LANES))
    for k in range(parts):
        row = place_ref[0] ^ k if len(pieces) > 1 else k
        piece = pieces[k] if len(pieces) > 1 else pieces[0].at[k * group:(k + 1) * group]
        rows_at = pl.ds(pl.multiple_of(row * group, group), group)
        hidden = []
        for tile in range(wide // LANES):
            at = slice(tile * LANES, (tile + 1) * LANES)
            value = piece[:, at].astype(jnp.float32) + bias_ref[...]
            half = 0.5 * (1.0 + lax.erf(value * 0.7071067811865476))
            hidden.append(value * half)
            slope_ref[rows_at, at] = half + value * jnp.exp(-0.5 * value * value) * 0.3989422804014327
        for j in range(blocks):
            tile, shift = divmod(j * STEP, LANES)
            block = hidden[tile]
            if shift:
                block = jnp.where(
                    lane < LANES - shift,
                    pltpu.roll(block, LANES - shift, 1),
                    pltpu.roll(hidden[tile + 1], LANES - shift, 1),
                )
            start = pl.multiple_of((row * blocks + j) * group, group)
            table_ref[pl.ds(start, group), :] = block.astype(jnp.bfloat16)


def activate(place, bias, block, parts, width):
    pieces = block if isinstance(block, list) else [block]
    group, wide = bias.shape[0], pieces[0].shape[1]
    blocks = -(-width // STEP)
    return pl.pallas_call(
        functools.partial(activate_kernel, parts, width),
        out_shape=[
            jax.ShapeDtypeStruct((parts * blocks * group, LANES), jnp.bfloat16),
            jax.ShapeDtypeStruct((parts * group, wide), jnp.float32),
        ],
        in_specs=[SMEM] + [VMEM] * (1 + len(pieces)),
        out_specs=[VMEM] * 2,
        compiler_params=PARAMS,
        cost_estimate=SMALL,
        name="activate",
    )(place, bias, *pieces)


def observe_kernel(parts, turns, width, place_ref, *refs):
    rows = parts * turns
    firsts, lasts, groups = refs[0:3], refs[3:6], refs[6:9]
    tables, slopes, refs = refs[9:9 + turns], refs[9 + turns:9 + 2 * turns], refs[9 + 2 * turns:]
    pieces, grads, refs = refs[:parts], refs[parts:parts + turns - 1], refs[parts + turns - 1:]
    departure_ref, table_ref, found_ref, obs_ref, spread_ref, first_ref, arrival = refs
    grads = [first_ref, *grads]
    group, wide = slopes[0].shape[0] // parts, slopes[0].shape[1]
    size = obs_ref.shape[2]
    blocks = -(-width // STEP)
    tiles = wide // LANES
    rem = width % LANES
    last = width // LANES
    lane = lane_iota((group, LANES))
    slab = blocks * group
    high = WINDOW * group

    copies, begin = [], 0
    for i, some in enumerate(groups):
        copies.append(pltpu.make_async_copy(some, obs_ref.at[pl.ds(begin, some.shape[0])], arrival.at[i]))
        begin += some.shape[0]
    for i, table in enumerate(tables):
        for lanes in range(2):
            start = (i * parts + 1 - lanes) * slab
            target = table_ref.at[pl.ds(start, parts * slab), pl.ds(lanes * LANES, LANES)]
            copies.append(pltpu.make_async_copy(table, target, arrival.at[3 + 2 * i + lanes]))
    for copy in copies:
        copy.start()
    for copy in copies:
        copy.wait()

    numbers = obs_ref.shape[0] * (size // OBS)
    lo_iota = lax.broadcasted_iota(jnp.int32, (LANES, OBS), 0)
    share = found_ref.shape[0] // (numbers // TOGETHER)

    def find(number):
        s = number // (size // OBS)
        at = pl.ds(pl.multiple_of(number % (size // OBS) * OBS, OBS), OBS)
        side = obs_ref[s, group:, at].astype(jnp.float32)
        whole = jnp.broadcast_to(side[4:5].astype(jnp.int32), (8, OBS))
        lowest = highest = begin = 0
        for low_ref, high_ref in zip(firsts, lasts):
            count = low_ref.shape[0]
            inside = jnp.clip(number - begin, 0, count - 1)
            lowest = jnp.where(number >= begin, low_ref[inside], lowest)
            highest = jnp.where(number >= begin, high_ref[inside], highest)
            begin += count
        lowest = jnp.clip(lowest, 0, (rows - 1) * blocks - 1)
        highest = jnp.clip(highest, lowest, (rows - 1) * blocks - 1)
        return s, at, side, whole, lowest, (highest - lowest) // WINDOW + 1

    @pl.loop(0, numbers // TOGETHER)
    def _(batch):
        start = pl.multiple_of(batch * share, share)
        found_ref[pl.ds(start, share), :] = jnp.zeros((share, 2 * LANES), jnp.float32)
        items, spreads = [find(batch * TOGETHER + i) for i in range(TOGETHER)], []
        for i, (_, _, side, _, _, _) in enumerate(items):
            low = side[5:6].astype(jnp.int32)
            first, second = lo_iota == low, lo_iota == low + 1
            spread = jnp.concatenate(
                [
                    jnp.where(first, side[0:1], jnp.where(second, side[1:2], 0.0)),
                    jnp.where(first, side[2:3], jnp.where(second, side[3:4], 0.0)),
                ],
                axis=0,
            ).astype(jnp.bfloat16)
            spread_ref[batch * TOGETHER + i] = spread
            spreads.append(spread)

        def gather(item, spread, window, model):
            _, _, _, whole, lowest, _ = item
            base = lowest + window * WINDOW
            at = pl.ds(pl.multiple_of((base + blocks) * group, group), high)
            part = jnp.dot(table_ref[at, :], spread, preferred_element_type=jnp.float32)
            for i in range(WINDOW):
                block = part[i * group:(i + 1) * group].reshape(group // 8, 8, OBS)
                model = jnp.where((whole == base + i)[None], block, model)
            return model

        zero = jnp.zeros((group // 8, 8, OBS), jnp.float32)
        models = [gather(item, spread, 0, zero) for item, spread in zip(items, spreads)]

        def more(window, models):
            return [
                gather(item, spread_ref[batch * TOGETHER + i], jnp.minimum(window, item[-1] - 1), model)
                for i, (item, model) in enumerate(zip(items, models))
            ]

        models = lax.fori_loop(1, functools.reduce(jnp.maximum, [item[-1] for item in items]), more, models)
        for (s, at, _, _, _, _), model in zip(items, models):
            departure = model.reshape(group, OBS) - obs_ref[s, :group, at].astype(jnp.float32)
            departure_ref[s, :, at] = departure.astype(jnp.bfloat16)

    @pl.loop(0, numbers // TOGETHER)
    def _(batch):
        items = [find(batch * TOGETHER + i) for i in range(TOGETHER)]

        def scatter(i, window):
            s, at, _, whole, lowest, _ = items[i]
            departure = departure_ref[s, :, at].astype(jnp.float32).reshape(group // 8, 8, OBS)
            base = lowest + window * WINDOW
            chosen = [
                jnp.where((whole == base + i)[None], departure, 0.0).reshape(group, OBS) for i in range(WINDOW)
            ]
            rows_at = pl.ds(pl.multiple_of(base * group, group), high)
            found_ref[rows_at, :] += lax.dot_general(
                jnp.concatenate(chosen, axis=0).astype(jnp.bfloat16),
                spread_ref[batch * TOGETHER + i],
                (((1,), (1,)), ((), ())),
                preferred_element_type=jnp.float32,
            )

        for i in range(TOGETHER):
            scatter(i, 0)
        for i in range(TOGETHER):
            pl.loop(1, items[i][-1])(functools.partial(scatter, i))

    for row in range(rows):
        out, slope = [ref.at[row % parts * group:(row % parts + 1) * group] for ref in (grads[row // parts], slopes[row // parts])]
        sums = [jnp.zeros((group, LANES), jnp.float32) for _ in range(tiles)]
        for j in range(blocks):
            tile, shift = divmod(j * STEP, LANES)
            block = jnp.zeros((group, LANES), jnp.float32)
            if row < rows - 1:
                start = (row * blocks + j) * group
                block += found_ref[start:start + group, :LANES]
            if row > 0:
                start = ((row - 1) * blocks + j) * group
                block += found_ref[start:start + group, LANES:]
            if shift:
                block = pltpu.roll(block, shift, 1)
                sums[tile] += jnp.where(lane >= shift, block, 0.0)
                sums[tile + 1] += jnp.where(lane < shift, block, 0.0)
            else:
                sums[tile] += block
        sums[0] += jnp.where(lane == 0, pltpu.roll(sums[last], LANES - rem, 1), 0.0)
        for tile in range(tiles):
            at = slice(tile * LANES, (tile + 1) * LANES)
            sums[tile] *= slope[:, at]
            if tile < last:
                out[:, at] = sums[tile].astype(jnp.bfloat16)
        out[:, last * LANES:] = wrapped_tail(sums[0], sums[last], rem).astype(jnp.bfloat16)
    for k, piece in enumerate(pieces):
        piece[...] = first_ref[pl.ds(pl.multiple_of((place_ref[0] ^ k) * group, group), group), :]


def observe(place, groups, tables, slopes, parts, width):
    group, wide = slopes[0].shape[0] // parts, slopes[0].shape[1]
    turns = len(slopes)
    rows = parts * turns
    blocks = -(-width // STEP)
    sets = sum(group[0].shape[0] for group in groups)
    depth, size = groups[0][0].shape[1:]
    numbers = sets * size // OBS
    found = -(-((rows - 1) * blocks + WINDOW) * group * TOGETHER // numbers // 8) * 8 * numbers // TOGETHER
    results = pl.pallas_call(
        functools.partial(observe_kernel, parts, turns, width),
        out_shape=[jax.ShapeDtypeStruct((group, wide), jnp.bfloat16)] * parts
        + [jax.ShapeDtypeStruct((parts * group, wide), jnp.bfloat16)] * (turns - 1)
        + [jax.ShapeDtypeStruct((sets, group, size), jnp.bfloat16)],
        in_specs=[SMEM] * 7 + [pl.BlockSpec(memory_space=pl.ANY)] * (3 + turns) + [VMEM] * turns,
        out_specs=[VMEM] * (parts + turns),
        scratch_shapes=[
            pltpu.VMEM(((rows + 1) * blocks * group, 2 * LANES), jnp.bfloat16),
            pltpu.VMEM((found, 2 * LANES), jnp.float32),
            pltpu.VMEM((sets, depth, size), jnp.bfloat16),
            pltpu.VMEM((numbers, 2 * LANES, OBS), jnp.bfloat16),
            pltpu.VMEM((parts * group, wide), jnp.bfloat16),
            pltpu.SemaphoreType.DMA((3 + 2 * turns,)),
        ],
        compiler_params=PARAMS,
        cost_estimate=SMALL,
        name="observe",
    )(place, *[some[i] for i in (2, 3, 0) for some in groups], *tables, *slopes)
    return [results[:parts], *results[parts:-1]], results[-1]


def after(value, *others):
    return lax.optimization_barrier((value, *others))[0]


def turn_over(block, axis):
    return lax.all_to_all(block, axis, split_axis=0, concat_axis=0, tiled=True)


def swap(pieces, axis):
    count = lax.axis_size(axis)
    return [pieces[0]] + [
        lax.ppermute(pieces[k], axis, [(i, i ^ k) for i in range(count)]) for k in range(1, count)
    ]


def mix(place, weights, blocks, ahead, between, beyond):
    count, turns = lax.axis_size("lat"), len(blocks)
    forward = [(i, i + 1) for i in range(count - 1)]
    backward = [(i + 1, i) for i in range(count - 1)]
    pieces = swap(blocks[0], "chan")
    heres = [after(assemble(place, pieces), *ahead)]
    for block in blocks[1:]:
        heres.append(turn_over(after(block, *pieces[1:]), "chan"))
    done = between(heres[0])
    if turns > 1:
        heres[1] = after(heres[1], *done)
    results, mixed, rest = [], (), ()
    for turn in range(turns):
        here = heres[turn]
        halos = [lax.ppermute(here, "lat", forward), lax.ppermute(here, "lat", backward)]
        ready = after(here, *mixed, *heres[turn + 1:turn + 2], *done, *rest)
        split = lax.axis_size("chan") if turn and turn == turns - 1 else 1
        mixed = conv(place, weights, halos[0], ready, halos[1], split)
        if split > 1:
            mixed = list(mixed)
            results.append(swap(mixed, "chan"))
        else:
            results.append(turn_over(after(mixed, *results[-1:]), "chan"))
            mixed = [mixed]
        if turn == 0:
            rest = beyond(mixed[0])
    return results, done, rest, mixed[0]


def shards(state, kernel, bias, innovations, interp, cells, counts):
    rows, width = state.shape[1:]
    parts, slabs = lax.axis_size("chan"), lax.axis_size("lat")
    total = kernel.shape[2]
    place, lat_place = lax.axis_index("chan").reshape(1), lax.axis_index("lat").reshape(1)
    forward_weights = kernel.reshape(3, 3 * total, total)
    backward_weights = jnp.transpose(kernel[::-1, ::-1], (0, 1, 3, 2)).reshape(3, 3 * total, total)

    blocks = split_rows(place, state, parts, padded_width(width))

    packed = pack_obs(after(counts, blocks[0][0]), innovations[:, 0], interp, cells, width)
    obs = turn_over(packed, "lat")
    quarter = slabs // 4
    mixed, one, two, last = mix(
        place, forward_weights, blocks, (obs,),
        lambda ahead: sort_obs(lat_place, after(obs, ahead), 0, quarter),
        lambda ahead: sort_obs(lat_place, after(obs, ahead), quarter, quarter),
    )
    three = sort_obs(lat_place, after(obs, last), 2 * quarter, 2 * quarter)

    tables, slopes = [], []
    for block in mixed:
        table, slope = activate(after(place, *tables), bias[:, None], block, parts, width)
        tables.append(table)
        slopes.append(slope)
    grads, departures = observe(place, [one, two, three], tables, slopes, parts, width)
    grad_blocks, low, high, last = mix(
        place, backward_weights, grads, (),
        lambda ahead: unsort_obs(after(departures, ahead), 0, [one[1], two[1]]),
        lambda ahead: unsort_obs(after(departures, ahead), 2 * quarter // JOIN, [three[1]]),
    )
    unsorted = lax.optimization_barrier((*low, *high, last))[:slabs]
    departures_out = unpack_obs(lat_place, swap(unsorted, "lat"))
    grad_state = join_rows(after(place, departures_out), grad_blocks, parts, width)
    return grad_state, departures_out.reshape(innovations.shape)


def solution(mesh):
    return jax.shard_map(
        shards,
        mesh=mesh,
        in_specs=(
            P("chan", "lat", None),
            P(),
            P("chan"),
            P("chan", "lat", None, None),
            P(None, "lat", None, None),
            P("lat", None, None),
            P("lat", None),
        ),
        out_specs=(P("chan", "lat", None), P("chan", "lat", None, None)),
        check_vma=False,
    )
```

```python
import functools

import jax
import jax.numpy as jnp
from jax import lax
from jax.experimental import pallas as pl
from jax.experimental.pallas import tpu as pltpu
from jax.sharding import PartitionSpec as P

SPACING = 8
LANES = 128
STEP = 120
TOGETHER = 4
WINDOW = 12
OBS = 256
SIDE = 16
JOIN = 2

VMEM = pl.BlockSpec(memory_space=pltpu.VMEM)
SMEM = pl.BlockSpec(memory_space=pltpu.SMEM)
CONV = pl.CostEstimate(flops=7 * 10**9, bytes_accessed=1000, transcendentals=0)
SMALL = pl.CostEstimate(flops=1000, bytes_accessed=1000, transcendentals=0)
PARAMS = pltpu.CompilerParams(vmem_limit_bytes=56 * 1024 * 1024)


def padded_width(width):
    return -(-(width + 3 * SPACING) // LANES) * LANES


def lane_iota(shape):
    return lax.broadcasted_iota(jnp.int32, shape, len(shape) - 1)


def wrapped_tail(first, tail, rem):
    lane = lane_iota(tail.shape)
    head = pltpu.roll(first, rem, 1)
    end = pltpu.roll(tail, LANES - rem, 1)
    out = jnp.where(lane < rem, tail, jnp.where(lane < rem + 2 * SPACING, head, 0.0))
    return jnp.where(lane >= LANES - SPACING, end, out)


def split_rows_kernel(parts, place_ref, state_ref, *refs):
    outs, rows_ref = refs[:-1], refs[-1]
    group, rows, width = state_ref.shape
    wide = outs[0].shape[1]
    main = width // LANES * LANES
    rem = width - main
    tiles = wide // LANES
    for tile in range(tiles):
        size = min(LANES, width - tile * LANES)
        part = state_ref[:, :, tile * LANES:tile * LANES + size].astype(jnp.float32)
        rows_ref[tile, :, :size] = part.reshape(group * rows, size)
    for number in range(rows):
        if number < parts:
            out, row = outs[number], place_ref[0] ^ number
        else:
            out, row = outs[parts - 1 + number // parts].at[number % parts * group:(number % parts + 1) * group], number
        strips = [rows_ref[tile, pl.ds(row, group, stride=rows), :] for tile in range(tiles)]
        for tile in range(tiles - 1):
            out[:, tile * LANES:(tile + 1) * LANES] = strips[tile].astype(jnp.bfloat16)
        out[:, main:] = wrapped_tail(strips[0], strips[-1], rem).astype(jnp.bfloat16)


def split_rows(place, state, parts, wide):
    group, rows, width = state.shape
    later = rows // parts - 1
    results = pl.pallas_call(
        functools.partial(split_rows_kernel, parts),
        out_shape=[jax.ShapeDtypeStruct((group, wide), jnp.bfloat16)] * parts
        + [jax.ShapeDtypeStruct((parts * group, wide), jnp.bfloat16)] * later,
        in_specs=[SMEM, VMEM],
        out_specs=[VMEM] * (parts + later),
        scratch_shapes=[pltpu.VMEM((wide // LANES, group * rows, LANES), jnp.float32)],
        compiler_params=PARAMS,
        cost_estimate=SMALL,
        name="split_rows",
    )(place, state)
    return [results[:parts], *results[parts:]]


def join_rows_kernel(parts, place_ref, *refs):
    pieces, out_ref, rows_ref = refs[:-2], refs[-2], refs[-1]
    group, rows, width = out_ref.shape
    for number in range(rows):
        turn, k = divmod(number, parts)
        if turn and turn == rows // parts - 1:
            piece, row = pieces[turn + k], turn * parts + (place_ref[0] ^ k)
        else:
            piece, row = pieces[turn].at[k * group:(k + 1) * group], number
        for tile in range(rows_ref.shape[0]):
            part = piece[:, tile * LANES:(tile + 1) * LANES].astype(jnp.float32)
            rows_ref[tile, pl.ds(row, group, stride=rows), :] = part
    for tile in range(rows_ref.shape[0]):
        size = min(LANES, width - tile * LANES)
        part = rows_ref[tile, :, :size].reshape(group, rows, size)
        out_ref[:, :, tile * LANES:tile * LANES + size] = part.astype(jnp.bfloat16)


def join_rows(place, blocks, parts, width):
    pieces = [piece for block in blocks for piece in (block if isinstance(block, list) else [block])]
    group, wide = blocks[0].shape[0] // parts, blocks[0].shape[1]
    rows = parts * len(blocks)
    return pl.pallas_call(
        functools.partial(join_rows_kernel, parts),
        out_shape=jax.ShapeDtypeStruct((group, rows, width), jnp.bfloat16),
        in_specs=[SMEM] + [VMEM] * len(pieces),
        out_specs=VMEM,
        scratch_shapes=[pltpu.VMEM((wide // LANES, group * rows, LANES), jnp.float32)],
        compiler_params=PARAMS,
        cost_estimate=SMALL,
        name="join_rows",
    )(place, *pieces)


def assemble_kernel(place_ref, *refs):
    pieces, out_ref = refs[:-1], refs[-1]
    group = pieces[0].shape[0]
    for k, piece in enumerate(pieces):
        start = pl.multiple_of((place_ref[0] ^ k) * group, group)
        out_ref[pl.ds(start, group), :] = piece[...]


def assemble(place, pieces):
    group, wide = pieces[0].shape
    return pl.pallas_call(
        assemble_kernel,
        out_shape=jax.ShapeDtypeStruct((group * len(pieces), wide), jnp.bfloat16),
        in_specs=[SMEM] + [VMEM] * len(pieces),
        out_specs=VMEM,
        compiler_params=PARAMS,
        cost_estimate=SMALL,
        name="assemble",
    )(place, *pieces)


def conv_kernel(place_ref, weights_ref, below_ref, here_ref, above_ref, *refs):
    outs, sums_ref = refs[:-1], refs[-1]
    total, wide = here_ref.shape
    columns = wide // 2 if wide % (4 * LANES) == 0 else LANES
    share = total // max(len(outs), 4)

    @pl.loop(0, wide // columns)
    def _(tile):
        at = pl.ds(pl.multiple_of(tile * columns, columns), columns)
        part = jnp.dot(weights_ref[1], here_ref[:, at], preferred_element_type=jnp.float32)
        part += jnp.dot(weights_ref[0], below_ref[:, at], preferred_element_type=jnp.float32)
        part += jnp.dot(weights_ref[2], above_ref[:, at], preferred_element_type=jnp.float32)
        sums_ref[:, at] = part

    for number in range(total // share):
        if len(outs) > 1:
            out, start = outs[number], pl.multiple_of((place_ref[0] ^ number) * share, share)
        else:
            out, start = outs[0].at[number * share:(number + 1) * share], number * share
        left = sums_ref[pl.ds(start, share), :]
        middle = sums_ref[pl.ds(start + total, share), :]
        right = sums_ref[pl.ds(start + 2 * total, share), :]
        mixed = middle + pltpu.roll(left, SPACING, 1) + pltpu.roll(right, wide - SPACING, 1)
        out[...] = mixed.astype(jnp.bfloat16)


def conv(place, weights, below, here, above, parts):
    total, wide = here.shape
    results = pl.pallas_call(
        conv_kernel,
        out_shape=[jax.ShapeDtypeStruct((total // parts, wide), jnp.bfloat16)] * parts,
        in_specs=[SMEM] + [VMEM] * 4,
        out_specs=[VMEM] * parts,
        scratch_shapes=[pltpu.VMEM((3 * total, wide), jnp.float32)],
        compiler_params=PARAMS,
        cost_estimate=CONV,
        name="conv",
    )(place, weights, below, here, above)
    return results if parts > 1 else results[0]


def pack_obs_kernel(width, counts_ref, values_ref, weights_ref, cells_ref, out_ref, tiles_ref):
    slabs, depth, slots = out_ref.shape
    group = depth - SIDE
    blocks = -(-width // STEP)
    for tile in range(slots // LANES):
        tiles_ref[tile] = values_ref[:, tile * LANES:(tile + 1) * LANES]
    all_weights = weights_ref[...].astype(jnp.float32)
    for slab in range(slabs):
        used = lane_iota((1, slots)) < counts_ref[0, slab]
        values = jnp.concatenate(
            [tiles_ref[tile, pl.ds(slab, group, stride=slabs), :] for tile in range(slots // LANES)], axis=1
        )
        out_ref[slab, :group, :] = jnp.where(used, values, 0.0).astype(jnp.bfloat16)
        weights = jnp.where(used, all_weights[:, 0, slab, :], 0.0)
        local = (cells_ref[0, slab:slab + 1, :] - slab * (SPACING * width)).astype(jnp.float32)
        row = jnp.clip(jnp.floor((local + 0.5) * (1.0 / width)), 0.0, SPACING - 2.0)
        column = local - row * width
        block = jnp.clip(jnp.floor((column + 0.5) * (1.0 / STEP)), 0.0, blocks - 1.0)
        side = jnp.concatenate(
            [weights, row * blocks + block, column - block * STEP, jnp.zeros((SIDE - 6, slots), jnp.float32)],
            axis=0,
        )
        out_ref[slab, group:, :] = side.astype(jnp.bfloat16)


def pack_obs(counts, values, weights, cells, width):
    group, slabs, slots = values.shape
    return pl.pallas_call(
        functools.partial(pack_obs_kernel, width),
        out_shape=jax.ShapeDtypeStruct((slabs, group + SIDE, slots), jnp.bfloat16),
        in_specs=[SMEM, VMEM, VMEM, VMEM],
        out_specs=VMEM,
        scratch_shapes=[pltpu.VMEM((slots // LANES, group * slabs, LANES), jnp.float32)],
        compiler_params=PARAMS,
        cost_estimate=SMALL,
        name="pack_obs",
    )(counts, values.reshape(group * slabs, slots), weights, cells)


def sort_obs_kernel(begin, place_ref, obs_ref, sorted_ref, rank_ref, first_ref, last_ref, joined_ref, column_ref):
    sets, depth, size = sorted_ref.shape
    group = depth - SIDE
    each = obs_ref.shape[2]
    for s in range(sets):
        for i in range(size // each):
            joined_ref[:, i * each:(i + 1) * each] = obs_ref[place_ref[0] ^ (begin + s * (size // each) + i)]
        which = joined_ref[group:, :].astype(jnp.float32)[4:5]
        key = which * size + lane_iota((1, size)).astype(jnp.float32)
        column_ref[...] = jnp.transpose(jnp.broadcast_to(key, (LANES, size)))
        ranks = []
        for tile in range(size // LANES):
            below = jnp.where(column_ref[...] < key[:, tile * LANES:(tile + 1) * LANES], 1.0, 0.0)
            ranks.append(jnp.sum(below, axis=0, keepdims=True))
        rank = jnp.concatenate(ranks, axis=1)
        rank_ref[s] = rank.astype(jnp.int32)
        column_ref[...] = jnp.transpose(jnp.broadcast_to(rank, (LANES, size)))

        @pl.loop(0, size // OBS)
        def _(tile):
            start = pl.multiple_of(tile * OBS, OBS)
            chosen = []
            for i in range(OBS // LANES):
                order = (lane_iota((1, LANES)) + (start + i * LANES)).astype(jnp.float32)
                chosen.append(jnp.where(column_ref[...] == order, 1.0, 0.0).astype(jnp.bfloat16))
            taken = jnp.dot(
                joined_ref[...], jnp.concatenate(chosen, axis=1), preferred_element_type=jnp.float32
            )
            sorted_ref[s, :, pl.ds(start, OBS)] = taken.astype(jnp.bfloat16)
            which = taken[group + 4:group + 5]
            first_ref[s * (size // OBS) + tile] = jnp.min(which).astype(jnp.int32)
            last_ref[s * (size // OBS) + tile] = jnp.max(which).astype(jnp.int32)


def sort_obs(place, obs, begin, slabs):
    depth, slots = obs.shape[1:]
    size = slots * JOIN
    sets = slabs // JOIN
    return pl.pallas_call(
        functools.partial(sort_obs_kernel, begin),
        out_shape=[
            jax.ShapeDtypeStruct((sets, depth, size), jnp.bfloat16),
            jax.ShapeDtypeStruct((sets, 1, size), jnp.int32),
            jax.ShapeDtypeStruct((sets * size // OBS,), jnp.int32),
            jax.ShapeDtypeStruct((sets * size // OBS,), jnp.int32),
        ],
        in_specs=[SMEM, VMEM],
        out_specs=[VMEM, VMEM, SMEM, SMEM],
        scratch_shapes=[pltpu.VMEM((depth, size), jnp.bfloat16), pltpu.VMEM((size, LANES), jnp.float32)],
        compiler_params=PARAMS,
        cost_estimate=SMALL,
        name="sort_obs",
    )(place, obs)


def unsort_obs_kernel(begin, count, sorted_ref, *refs):
    ranks, outs = refs[:-count], refs[-count:]
    size = sorted_ref.shape[2]
    each = outs[0].shape[1]
    places = [(rank_ref, s) for rank_ref in ranks for s in range(rank_ref.shape[0])]
    for number, out in enumerate(outs):
        s, offset = divmod(number * each, size)

        @pl.loop(0, each // OBS)
        def _(tile):
            start = pl.multiple_of(tile * OBS, OBS)
            rank = places[s][0][places[s][1], :, pl.ds(offset + start, OBS)]
            chosen = jnp.where(lax.broadcasted_iota(jnp.int32, (size, OBS), 0) == rank, 1.0, 0.0)
            taken = jnp.dot(
                sorted_ref[begin + s], chosen.astype(jnp.bfloat16), preferred_element_type=jnp.float32
            )
            out[:, pl.ds(start, OBS)] = taken.astype(jnp.bfloat16)


def unsort_obs(values, begin, ranks):
    group, size = values.shape[1:]
    count = sum(rank.shape[0] for rank in ranks) * JOIN
    return pl.pallas_call(
        functools.partial(unsort_obs_kernel, begin, count),
        out_shape=[jax.ShapeDtypeStruct((group, size // JOIN), jnp.bfloat16)] * count,
        in_specs=[VMEM] * (1 + len(ranks)),
        out_specs=[VMEM] * count,
        compiler_params=PARAMS,
        cost_estimate=SMALL,
        name="unsort_obs",
    )(values, *ranks)


def unpack_obs_kernel(place_ref, *refs):
    pieces, out_ref, tiles_ref = refs[:-2], refs[-2], refs[-1]
    slabs = len(pieces)
    group, slots = pieces[0].shape
    for k, piece in enumerate(pieces):
        slab = place_ref[0] ^ k
        for tile in range(slots // LANES):
            part = piece[:, tile * LANES:(tile + 1) * LANES].astype(jnp.float32)
            tiles_ref[tile, pl.ds(slab, group, stride=slabs), :] = part
    for tile in range(slots // LANES):
        out_ref[:, tile * LANES:(tile + 1) * LANES] = tiles_ref[tile]


def unpack_obs(place, pieces):
    slabs = len(pieces)
    group, slots = pieces[0].shape
    return pl.pallas_call(
        unpack_obs_kernel,
        out_shape=jax.ShapeDtypeStruct((group * slabs, slots), jnp.float32),
        in_specs=[SMEM] + [VMEM] * slabs,
        out_specs=VMEM,
        scratch_shapes=[pltpu.VMEM((slots // LANES, group * slabs, LANES), jnp.float32)],
        compiler_params=PARAMS,
        cost_estimate=SMALL,
        name="unpack_obs",
    )(place, *pieces)


def activate_kernel(parts, width, place_ref, bias_ref, *refs):
    pieces, table_ref, slope_ref = refs[:-2], refs[-2], refs[-1]
    blocks = -(-width // STEP)
    group, wide = slope_ref.shape[0] // parts, slope_ref.shape[1]
    lane = lane_iota((group, LANES))
    for k in range(parts):
        row = place_ref[0] ^ k if len(pieces) > 1 else k
        piece = pieces[k] if len(pieces) > 1 else pieces[0].at[k * group:(k + 1) * group]
        rows_at = pl.ds(pl.multiple_of(row * group, group), group)
        hidden = []
        for tile in range(wide // LANES):
            at = slice(tile * LANES, (tile + 1) * LANES)
            value = piece[:, at].astype(jnp.float32) + bias_ref[...]
            half = 0.5 * (1.0 + lax.erf(value * 0.7071067811865476))
            hidden.append(value * half)
            slope_ref[rows_at, at] = half + value * jnp.exp(-0.5 * value * value) * 0.3989422804014327
        for j in range(blocks):
            tile, shift = divmod(j * STEP, LANES)
            block = hidden[tile]
            if shift:
                block = jnp.where(
                    lane < LANES - shift,
                    pltpu.roll(block, LANES - shift, 1),
                    pltpu.roll(hidden[tile + 1], LANES - shift, 1),
                )
            start = pl.multiple_of((row * blocks + j) * group, group)
            table_ref[pl.ds(start, group), :] = block.astype(jnp.bfloat16)


def activate(place, bias, block, parts, width):
    pieces = block if isinstance(block, list) else [block]
    group, wide = bias.shape[0], pieces[0].shape[1]
    blocks = -(-width // STEP)
    return pl.pallas_call(
        functools.partial(activate_kernel, parts, width),
        out_shape=[
            jax.ShapeDtypeStruct((parts * blocks * group, LANES), jnp.bfloat16),
            jax.ShapeDtypeStruct((parts * group, wide), jnp.float32),
        ],
        in_specs=[SMEM] + [VMEM] * (1 + len(pieces)),
        out_specs=[VMEM] * 2,
        compiler_params=PARAMS,
        cost_estimate=SMALL,
        name="activate",
    )(place, bias, *pieces)


def observe_kernel(parts, turns, width, place_ref, *refs):
    rows = parts * turns
    firsts, lasts, groups = refs[0:3], refs[3:6], refs[6:9]
    tables, slopes, refs = refs[9:9 + turns], refs[9 + turns:9 + 2 * turns], refs[9 + 2 * turns:]
    pieces, grads, refs = refs[:parts], refs[parts:parts + turns - 1], refs[parts + turns - 1:]
    departure_ref, table_ref, found_ref, obs_ref, spread_ref, first_ref, arrival = refs
    grads = [first_ref, *grads]
    group, wide = slopes[0].shape[0] // parts, slopes[0].shape[1]
    size = obs_ref.shape[2]
    blocks = -(-width // STEP)
    tiles = wide // LANES
    rem = width % LANES
    last = width // LANES
    lane = lane_iota((group, LANES))
    slab = blocks * group
    high = WINDOW * group

    copies, begin = [], 0
    for i, some in enumerate(groups):
        copies.append(pltpu.make_async_copy(some, obs_ref.at[pl.ds(begin, some.shape[0])], arrival.at[i]))
        begin += some.shape[0]
    for i, table in enumerate(tables):
        for lanes in range(2):
            start = (i * parts + 1 - lanes) * slab
            target = table_ref.at[pl.ds(start, parts * slab), pl.ds(lanes * LANES, LANES)]
            copies.append(pltpu.make_async_copy(table, target, arrival.at[3 + 2 * i + lanes]))
    for copy in copies:
        copy.start()
    for copy in copies:
        copy.wait()

    numbers = obs_ref.shape[0] * (size // OBS)
    lo_iota = lax.broadcasted_iota(jnp.int32, (LANES, OBS), 0)
    share = found_ref.shape[0] // (numbers // TOGETHER)

    def find(number):
        s = number // (size // OBS)
        at = pl.ds(pl.multiple_of(number % (size // OBS) * OBS, OBS), OBS)
        side = obs_ref[s, group:, at].astype(jnp.float32)
        whole = jnp.broadcast_to(side[4:5].astype(jnp.int32), (8, OBS))
        lowest = highest = begin = 0
        for low_ref, high_ref in zip(firsts, lasts):
            count = low_ref.shape[0]
            inside = jnp.clip(number - begin, 0, count - 1)
            lowest = jnp.where(number >= begin, low_ref[inside], lowest)
            highest = jnp.where(number >= begin, high_ref[inside], highest)
            begin += count
        lowest = jnp.clip(lowest, 0, (rows - 1) * blocks - 1)
        highest = jnp.clip(highest, lowest, (rows - 1) * blocks - 1)
        return s, at, side, whole, lowest, (highest - lowest) // WINDOW + 1

    @pl.loop(0, numbers // TOGETHER)
    def _(batch):
        start = pl.multiple_of(batch * share, share)
        found_ref[pl.ds(start, share), :] = jnp.zeros((share, 2 * LANES), jnp.float32)
        items, spreads = [find(batch * TOGETHER + i) for i in range(TOGETHER)], []
        for i, (_, _, side, _, _, _) in enumerate(items):
            low = side[5:6].astype(jnp.int32)
            first, second = lo_iota == low, lo_iota == low + 1
            spread = jnp.concatenate(
                [
                    jnp.where(first, side[0:1], jnp.where(second, side[1:2], 0.0)),
                    jnp.where(first, side[2:3], jnp.where(second, side[3:4], 0.0)),
                ],
                axis=0,
            ).astype(jnp.bfloat16)
            spread_ref[batch * TOGETHER + i] = spread
            spreads.append(spread)

        def gather(item, spread, window, model):
            _, _, _, whole, lowest, _ = item
            base = lowest + window * WINDOW
            at = pl.ds(pl.multiple_of((base + blocks) * group, group), high)
            part = jnp.dot(table_ref[at, :], spread, preferred_element_type=jnp.float32)
            for i in range(WINDOW):
                block = part[i * group:(i + 1) * group].reshape(group // 8, 8, OBS)
                model = jnp.where((whole == base + i)[None], block, model)
            return model

        zero = jnp.zeros((group // 8, 8, OBS), jnp.float32)
        models = [gather(item, spread, 0, zero) for item, spread in zip(items, spreads)]

        def more(window, models):
            return [
                gather(item, spread_ref[batch * TOGETHER + i], jnp.minimum(window, item[-1] - 1), model)
                for i, (item, model) in enumerate(zip(items, models))
            ]

        models = lax.fori_loop(1, functools.reduce(jnp.maximum, [item[-1] for item in items]), more, models)
        for (s, at, _, _, _, _), model in zip(items, models):
            departure = model.reshape(group, OBS) - obs_ref[s, :group, at].astype(jnp.float32)
            departure_ref[s, :, at] = departure.astype(jnp.bfloat16)

    @pl.loop(0, numbers // TOGETHER)
    def _(batch):
        items = [find(batch * TOGETHER + i) for i in range(TOGETHER)]

        def scatter(i, window):
            s, at, _, whole, lowest, _ = items[i]
            departure = departure_ref[s, :, at].astype(jnp.float32).reshape(group // 8, 8, OBS)
            base = lowest + window * WINDOW
            chosen = [
                jnp.where((whole == base + i)[None], departure, 0.0).reshape(group, OBS) for i in range(WINDOW)
            ]
            rows_at = pl.ds(pl.multiple_of(base * group, group), high)
            found_ref[rows_at, :] += lax.dot_general(
                jnp.concatenate(chosen, axis=0).astype(jnp.bfloat16),
                spread_ref[batch * TOGETHER + i],
                (((1,), (1,)), ((), ())),
                preferred_element_type=jnp.float32,
            )

        for i in range(TOGETHER):
            scatter(i, 0)
        for i in range(TOGETHER):
            pl.loop(1, items[i][-1])(functools.partial(scatter, i))

    for row in range(rows):
        out, slope = [ref.at[row % parts * group:(row % parts + 1) * group] for ref in (grads[row // parts], slopes[row // parts])]
        sums = [jnp.zeros((group, LANES), jnp.float32) for _ in range(tiles)]
        for j in range(blocks):
            tile, shift = divmod(j * STEP, LANES)
            block = jnp.zeros((group, LANES), jnp.float32)
            if row < rows - 1:
                start = (row * blocks + j) * group
                block += found_ref[start:start + group, :LANES]
            if row > 0:
                start = ((row - 1) * blocks + j) * group
                block += found_ref[start:start + group, LANES:]
            if shift:
                block = pltpu.roll(block, shift, 1)
                sums[tile] += jnp.where(lane >= shift, block, 0.0)
                sums[tile + 1] += jnp.where(lane < shift, block, 0.0)
            else:
                sums[tile] += block
        sums[0] += jnp.where(lane == 0, pltpu.roll(sums[last], LANES - rem, 1), 0.0)
        for tile in range(tiles):
            at = slice(tile * LANES, (tile + 1) * LANES)
            sums[tile] *= slope[:, at]
            if tile < last:
                out[:, at] = sums[tile].astype(jnp.bfloat16)
        out[:, last * LANES:] = wrapped_tail(sums[0], sums[last], rem).astype(jnp.bfloat16)
    for k, piece in enumerate(pieces):
        piece[...] = first_ref[pl.ds(pl.multiple_of((place_ref[0] ^ k) * group, group), group), :]


def observe(place, groups, tables, slopes, parts, width):
    group, wide = slopes[0].shape[0] // parts, slopes[0].shape[1]
    turns = len(slopes)
    rows = parts * turns
    blocks = -(-width // STEP)
    sets = sum(group[0].shape[0] for group in groups)
    depth, size = groups[0][0].shape[1:]
    numbers = sets * size // OBS
    found = -(-((rows - 1) * blocks + WINDOW) * group * TOGETHER // numbers // 8) * 8 * numbers // TOGETHER
    results = pl.pallas_call(
        functools.partial(observe_kernel, parts, turns, width),
        out_shape=[jax.ShapeDtypeStruct((group, wide), jnp.bfloat16)] * parts
        + [jax.ShapeDtypeStruct((parts * group, wide), jnp.bfloat16)] * (turns - 1)
        + [jax.ShapeDtypeStruct((sets, group, size), jnp.bfloat16)],
        in_specs=[SMEM] * 7 + [pl.BlockSpec(memory_space=pl.ANY)] * (3 + turns) + [VMEM] * turns,
        out_specs=[VMEM] * (parts + turns),
        scratch_shapes=[
            pltpu.VMEM(((rows + 1) * blocks * group, 2 * LANES), jnp.bfloat16),
            pltpu.VMEM((found, 2 * LANES), jnp.float32),
            pltpu.VMEM((sets, depth, size), jnp.bfloat16),
            pltpu.VMEM((numbers, 2 * LANES, OBS), jnp.bfloat16),
            pltpu.VMEM((parts * group, wide), jnp.bfloat16),
            pltpu.SemaphoreType.DMA((3 + 2 * turns,)),
        ],
        compiler_params=PARAMS,
        cost_estimate=SMALL,
        name="observe",
    )(place, *[some[i] for i in (2, 3, 0) for some in groups], *tables, *slopes)
    return [results[:parts], *results[parts:-1]], results[-1]


def after(value, *others):
    return lax.optimization_barrier((value, *others))[0]


def turn_over(block, axis):
    return lax.all_to_all(block, axis, split_axis=0, concat_axis=0, tiled=True)


def swap(pieces, axis):
    count = lax.axis_size(axis)
    return [pieces[0]] + [
        lax.ppermute(pieces[k], axis, [(i, i ^ k) for i in range(count)]) for k in range(1, count)
    ]


def mix(place, weights, blocks, ahead, between, beyond):
    count, turns = lax.axis_size("lat"), len(blocks)
    forward = [(i, i + 1) for i in range(count - 1)]
    backward = [(i + 1, i) for i in range(count - 1)]
    pieces = swap(blocks[0], "chan")
    heres = [after(assemble(place, pieces), *ahead)]
    for block in blocks[1:]:
        heres.append(turn_over(after(block, *pieces[1:]), "chan"))
    done = between(heres[0])
    if turns > 1:
        heres[1] = after(heres[1], *done)
    results, mixed, rest = [], (), ()
    for turn in range(turns):
        here = heres[turn]
        halos = [lax.ppermute(here, "lat", forward), lax.ppermute(here, "lat", backward)]
        ready = after(here, *mixed, *heres[turn + 1:turn + 2], *done, *rest)
        split = lax.axis_size("chan") if turn and turn == turns - 1 else 1
        mixed = conv(place, weights, halos[0], ready, halos[1], split)
        if split > 1:
            mixed = list(mixed)
            results.append(swap(mixed, "chan"))
        else:
            results.append(turn_over(after(mixed, *results[-1:]), "chan"))
            mixed = [mixed]
        if turn == 0:
            rest = beyond(mixed[0])
    return results, done, rest, mixed[0]


def shards(state, kernel, bias, innovations, interp, cells, counts):
    rows, width = state.shape[1:]
    parts, slabs = lax.axis_size("chan"), lax.axis_size("lat")
    total = kernel.shape[2]
    place, lat_place = lax.axis_index("chan").reshape(1), lax.axis_index("lat").reshape(1)
    forward_weights = kernel.reshape(3, 3 * total, total)
    backward_weights = jnp.transpose(kernel[::-1, ::-1], (0, 1, 3, 2)).reshape(3, 3 * total, total)

    blocks = split_rows(place, state, parts, padded_width(width))

    packed = pack_obs(after(counts, blocks[0][0]), innovations[:, 0], interp, cells, width)
    obs = turn_over(packed, "lat")
    quarter = slabs // 4
    mixed, one, two, last = mix(
        place, forward_weights, blocks, (obs,),
        lambda ahead: sort_obs(lat_place, after(obs, ahead), 0, quarter),
        lambda ahead: sort_obs(lat_place, after(obs, ahead), quarter, quarter),
    )
    three = sort_obs(lat_place, after(obs, last), 2 * quarter, 2 * quarter)

    tables, slopes = [], []
    for block in mixed:
        table, slope = activate(after(place, *tables), bias[:, None], block, parts, width)
        tables.append(table)
        slopes.append(slope)
    grads, departures = observe(place, [one, two, three], tables, slopes, parts, width)
    grad_blocks, low, high, last = mix(
        place, backward_weights, grads, (),
        lambda ahead: unsort_obs(after(departures, ahead), 0, [one[1], two[1]]),
        lambda ahead: unsort_obs(after(departures, ahead), 2 * quarter // JOIN, [three[1]]),
    )
    unsorted = lax.optimization_barrier((*low, *high, last))[:slabs]
    departures_out = unpack_obs(lat_place, swap(unsorted, "lat"))
    grad_state = join_rows(after(place, departures_out), grad_blocks, parts, width)
    return grad_state, departures_out.reshape(innovations.shape)


def solution(mesh):
    return jax.shard_map(
        shards,
        mesh=mesh,
        in_specs=(
            P("chan", "lat", None),
            P(),
            P("chan"),
            P("chan", "lat", None, None),
            P(None, "lat", None, None),
            P("lat", None, None),
            P("lat", None),
        ),
        out_specs=(P("chan", "lat", None), P("chan", "lat", None, None)),
        check_vma=False,
    )
```
